32 devices in a mesh: inner: 4 (over y, x), blk: 8 (over z, core).
Axes of the slice: x: 2, y: 2, z: 4, core: 2. Of those that a mesh axis runs over, the one named last changes fastest.
Arguments:
- image_emb: float32 [768, 768], P(('inner', 'blk')), may hold values from -150 to 150
- text_emb: float32 [768, 768], P(('inner', 'blk')), may hold values from -150 to 150
- logit_scale: float32 [1], replicated, may hold values from 30 to 100
Outputs:
- mean_loss: float32 [1], replicated
- image_grad: float32 [768, 768], P(('inner', 'blk'))
- text_grad: float32 [768, 768], P(('inner', 'blk'))
The draws below stay inside these ranges and needn't reach their ends.
All inputs are finite; a program needn't handle non-finite values.
Results may differ from the reference program's by a relative error of at most 0.006.
Values may be sent and summed in bfloat16 or wider, within the bound.
A program may use at most 64 MiB of HBM per device.

```python
import jax
import jax.numpy as jnp
from jax import lax

E = 768
BATCH = 768


def embed_pair(key):
    keys = jax.random.split(jax.random.fold_in(key, 4242), 5)
    image_noise = jax.random.truncated_normal(keys[0], -5.0, 5.0, (BATCH, E), jnp.float32)
    text_noise = jax.random.truncated_normal(keys[1], -5.0, 5.0, (BATCH, E), jnp.float32)
    image_spread = jnp.exp(jax.random.uniform(keys[3], (BATCH, 1), jnp.float32) * jnp.log(10.0))
    text_spread = jnp.exp(jax.random.uniform(keys[4], (BATCH, 1), jnp.float32) * jnp.log(10.0))
    image_rows = image_noise
    text_rows = text_noise
    return (image_rows * image_spread, text_rows * text_spread)


def draw_image_emb(key, part):
    return embed_pair(key)[0]


def draw_text_emb(key, part):
    return embed_pair(key)[1]


def draw_logit_scale(key, part):
    sample = jax.random.uniform(jax.random.fold_in(key, 99), (1,), jnp.float32)
    return jnp.exp(jnp.log(30.0) + sample * jnp.log(100.0 / 30.0))


def setup_inputs(seed: int = 0) -> dict:
    splits = jax.random.split(jax.random.key(seed), 4)
    return {
        "image_emb": draw_image_emb(jax.random.fold_in(splits[3], 71), 0),
        "text_emb": draw_text_emb(jax.random.fold_in(splits[3], 71), 0),
        "logit_scale": draw_logit_scale(jax.random.fold_in(splits[3], 71), 0),
    }


EPSILON = 1e-06

def unit_rows(values):
    inverse = lax.rsqrt(lax.optimization_barrier(jnp.sum(values * values, axis=1, keepdims=True)) + EPSILON)
    return (values * inverse, inverse)

def project(gradient, direction, inverse):
    return (gradient - direction * lax.optimization_barrier(jnp.sum(gradient * direction, axis=1, keepdims=True))) * inverse

def reference(image_emb, text_emb, logit_scale):
    factor = logit_scale[0]
    image_unit, image_inverse = unit_rows(image_emb)
    text_unit, text_inverse = unit_rows(text_emb)
    image_half = image_unit.astype(jnp.bfloat16)
    text_half = text_unit.astype(jnp.bfloat16)
    count_rows = image_emb.shape[0]
    embed_width = image_emb.shape[1]
    text_blocks = text_half.reshape(16, count_rows // 16, embed_width)

    def scores(text_block):
        return factor * jnp.dot(image_half, text_block.T, preferred_element_type=jnp.float32)

    def stats_step(state, text_block):
        row_peak, row_total = state
        logits = scores(text_block)
        new_peak = jnp.maximum(row_peak, lax.optimization_barrier(jnp.max(logits, axis=1)))
        row_total = row_total * jnp.exp(row_peak - new_peak) + lax.optimization_barrier(jnp.sum(jnp.exp(logits - new_peak[:, None]), axis=1))
        col_peak = lax.optimization_barrier(jnp.max(logits, axis=0))
        col_lse = col_peak + jnp.log(lax.optimization_barrier(jnp.sum(jnp.exp(logits - col_peak[None, :]), axis=0)))
        return ((new_peak, row_total), col_lse)
    initial = (jnp.full((count_rows,), -1e+30, jnp.float32), jnp.zeros((count_rows,), jnp.float32))
    (row_peak, row_total), col_parts = lax.scan(stats_step, initial, text_blocks)
    row_lse = row_peak + jnp.log(row_total)
    col_lse = col_parts.reshape(count_rows)

    def grad_step(image_acc, inputs):
        text_block, col_block = inputs
        logits = scores(text_block)
        weights = (0.5 * factor * (jnp.exp(logits - row_lse[:, None]) + jnp.exp(logits - col_block[None, :]))).astype(jnp.bfloat16)
        image_acc = image_acc + jnp.dot(weights, text_block, preferred_element_type=jnp.float32)
        text_part = jnp.dot(weights.T, image_half, preferred_element_type=jnp.float32)
        return (image_acc, text_part)
    image_sum, text_parts = lax.scan(grad_step, jnp.zeros((count_rows, embed_width), jnp.float32), (text_blocks, col_lse.reshape(16, count_rows // 16)))
    text_sum = text_parts.reshape(count_rows, embed_width)
    diagonal = factor * lax.optimization_barrier(jnp.sum(image_half.astype(jnp.float32) * text_half.astype(jnp.float32), axis=1))
    mean_loss = (jnp.sum(row_lse - diagonal) + jnp.sum(col_lse - diagonal)) / (2.0 * count_rows)
    image_pull = image_sum - factor * text_half.astype(jnp.float32)
    text_pull = text_sum - factor * image_half.astype(jnp.float32)
    return (mean_loss.reshape(1), project(image_pull, image_unit, image_inverse), project(text_pull, text_unit, text_inverse))
```

```python
import functools

import jax
import jax.numpy as jnp
from jax import lax
from jax.experimental import pallas as pl
from jax.experimental.pallas import tpu as pltpu
from jax.sharding import PartitionSpec as P

EPSILON = 1e-06
MESH = pl.DeviceIdType.MESH


def unit_rows(values):
    inverse = lax.rsqrt(jnp.sum(values * values, axis=1, keepdims=True) + EPSILON)
    return (values * inverse, inverse)


def project(gradient, direction, inverse):
    return (gradient - direction * jnp.sum(gradient * direction, axis=1, keepdims=True)) * inverse


class Group:
    def __init__(self, me, size, device_of, order, sems):
        self.me, self.size, self.device_of, self.sems = me, size, device_of, sems
        self.order = order

    def others(self, reverse=False):
        steps = range(1, self.size)
        return [self.order(self.me, self.size, k) for k in (reversed(steps) if reverse else steps)]

    def copy(self, src, dst, stage, to):
        send_sems, recv_sems = self.sems
        return pltpu.make_async_remote_copy(
            src_ref=src,
            dst_ref=dst,
            send_sem=send_sems.at[stage],
            recv_sem=recv_sems.at[stage],
            device_id=self.device_of(to),
            device_id_type=MESH,
        )

    def whole(self, buf, stage):
        part = buf.at[pl.ds(0, self.size - 1)]
        return self.copy(part, part, stage, self.order(self.me, self.size, 1))

    def start_gather(self, buf, stage, reverse=False):
        mine = buf.at[self.me]
        for to in self.others(reverse):
            self.copy(mine, mine, stage, to).start()

    def wait_recv(self, buf, stage):
        self.whole(buf, stage).wait_recv()

    def wait_send(self, buf, stage):
        self.whole(buf, stage).wait_send()

    def start_scatter(self, parts, slots, stage, reverse=False):
        for to in self.others(reverse):
            self.copy(parts.at[to], slots.at[self.me], stage, to).start()


def ascending(me, size, k):
    return k - 1 + (k - 1 >= me).astype(jnp.int32)


def flipped(me, size, k):
    if size & (size - 1):
        return lax.rem(me + k, size)
    out, bit = me, 1
    while bit <= k:
        if k & bit:
            out = out + bit * (1 - 2 * lax.rem(me // bit, 2))
        bit *= 2
    return out


def as_column(row):
    size = row.shape[1]
    shape = (size, size)
    same = lax.broadcasted_iota(jnp.int32, shape, 0) == lax.broadcasted_iota(jnp.int32, shape, 1)
    return jnp.sum(jnp.where(same, row, 0.0), axis=1, keepdims=True)


def as_row(column):
    size = column.shape[0]
    shape = (size, size)
    same = lax.broadcasted_iota(jnp.int32, shape, 0) == lax.broadcasted_iota(jnp.int32, shape, 1)
    return jnp.sum(jnp.where(same, column, 0.0), axis=0, keepdims=True)


def merge(stats):
    highest = jnp.max(stats[:, 0:1, :], axis=0)
    total = jnp.sum(stats[:, 1:2, :] * jnp.exp(stats[:, 0:1, :] - highest[None]), axis=0)
    return highest + jnp.log(total)


def flat_half(blocks):
    count, rows, width = blocks.shape
    return blocks.astype(jnp.float32).reshape(count * rows, width).astype(jnp.bfloat16)


def kernel(
    inner_count,
    line_count,
    pair_count,
    scale_ref,
    image_hbm,
    text_hbm,
    packed_ref,
    images,
    texts,
    row_stats,
    col_stats,
    row_sums,
    col_sums,
    image_parts,
    text_parts,
    image_slots,
    text_slots,
    image_own,
    text_own,
    image_ref,
    text_ref,
    input_sems,
    line_send,
    line_recv,
    plane_send,
    plane_recv,
):
    text_in = pltpu.make_async_copy(text_hbm, text_ref, input_sems.at[0])
    image_in = pltpu.make_async_copy(image_hbm, image_ref, input_sems.at[1])
    text_in.start()
    image_in.start()
    inner, blk = lax.axis_index("inner"), lax.axis_index("blk")
    place, side = blk // pair_count, lax.rem(blk, pair_count)
    line = Group(
        place,
        line_count,
        lambda z: (inner, z * pair_count + side),
        ascending,
        (line_send, line_recv),
    )
    plane = Group(
        inner * pair_count + side,
        inner_count * pair_count,
        lambda g: (g // pair_count, place * pair_count + lax.rem(g, pair_count)),
        flipped,
        (plane_send, plane_recv),
    )
    groups = (plane, line)
    barrier = pltpu.get_barrier_semaphore()
    for group in groups:
        for to in group.others():
            pl.semaphore_signal(
                barrier, inc=1, device_id=group.device_of(to), device_id_type=MESH
            )

    factor = scale_ref[0]
    text_in.wait()
    text_unit, text_inverse = unit_rows(text_ref[...])
    text_half = text_unit.astype(jnp.bfloat16)
    texts[plane.me] = text_half
    image_in.wait()
    image_unit, image_inverse = unit_rows(image_ref[...])
    image_half = image_unit.astype(jnp.bfloat16)
    images[line.me] = image_half
    pl.semaphore_wait(barrier, plane.size + line.size - 2)
    line.start_gather(images, 0, reverse=True)
    plane.start_gather(texts, 0, reverse=True)
    image_back = image_half.astype(jnp.float32)
    text_back = text_half.astype(jnp.float32)
    diagonal = factor * jnp.sum(image_back * text_back)
    plane.wait_recv(texts, 0)
    line.wait_recv(images, 0)

    image_group = flat_half(images[...])
    text_group = flat_half(texts[...])
    image_count, text_count = image_group.shape[0], text_group.shape[0]
    logits = factor * lax.dot_general(
        image_group, text_group, (((1,), (1,)), ((), ())), preferred_element_type=jnp.float32
    )
    row_peak = jnp.max(logits, axis=1, keepdims=True)
    row_total = jnp.sum(jnp.exp(logits - row_peak), axis=1, keepdims=True)
    col_peak = jnp.max(logits, axis=0, keepdims=True)
    col_total = jnp.sum(jnp.exp(logits - col_peak), axis=0, keepdims=True)
    row_stats[line.me, 0:1, :] = as_row(row_peak)
    row_stats[line.me, 1:2, :] = as_row(row_total)
    col_stats[plane.me, 0:1, :] = col_peak
    col_stats[plane.me, 1:2, :] = col_total
    col_stats[plane.me, 2:3, :] = jnp.full((1, text_count), diagonal, jnp.float32)
    line.start_gather(row_stats, 1)
    plane.start_gather(col_stats, 1, reverse=True)
    line.wait_recv(row_stats, 1)
    plane.wait_recv(col_stats, 1)
    row_lse = merge(row_stats[...])
    col_lse = merge(col_stats[...])

    tile = row_sums.shape[1:]
    plane_diagonal = jnp.sum(col_stats[:, 2, 0:1])
    row_sums[plane.me] = jnp.full(tile, jnp.sum(row_lse), jnp.float32)
    col_sums[line.me] = jnp.full(tile, jnp.sum(col_lse) - 2.0 * plane_diagonal, jnp.float32)
    plane.start_gather(row_sums, 3)
    line.start_gather(col_sums, 3)

    weights = (
        0.5 * factor * (jnp.exp(logits - as_column(row_lse)) + jnp.exp(logits - col_lse))
    ).astype(jnp.bfloat16)
    image_own[...] = jnp.dot(
        weights, text_group, preferred_element_type=jnp.float32
    ).reshape(image_parts.shape)
    image_parts[...] = image_own[...].astype(jnp.bfloat16)
    line.start_scatter(image_parts, image_slots, 2)
    text_own[...] = lax.dot_general(
        weights, image_group, (((0,), (0,)), ((), ())), preferred_element_type=jnp.float32
    ).reshape(text_parts.shape)
    text_parts[...] = text_own[...].astype(jnp.bfloat16)
    plane.start_scatter(text_parts, text_slots, 2)

    rows = image_ref.shape[0]
    plane.wait_recv(text_slots, 2)
    text_sum = text_own[plane.me]
    for other in plane.others():
        text_sum = text_sum + text_slots[other].astype(jnp.float32)
    packed_ref[pl.ds(rows, rows)] = project(text_sum - factor * image_back, text_unit, text_inverse)
    line.wait_recv(image_slots, 2)
    image_sum = image_own[line.me]
    for other in line.others():
        image_sum = image_sum + image_slots[other].astype(jnp.float32)
    packed_ref[pl.ds(0, rows)] = project(image_sum - factor * text_back, image_unit, image_inverse)

    plane.wait_recv(row_sums, 3)
    line.wait_recv(col_sums, 3)
    examples = 2.0 * line.size * plane.size * rows
    whole = jnp.sum(row_sums[...], axis=0)[0:1, 0:1] + jnp.sum(col_sums[...], axis=0)[0:1, 0:1]
    packed_ref[pl.ds(2 * rows, 8)] = jnp.broadcast_to(whole / examples, (8, packed_ref.shape[1]))
    for buf_line, buf_plane, stage in (
        (images, texts, 0),
        (row_stats, col_stats, 1),
        (image_parts, text_parts, 2),
        (col_sums, row_sums, 3),
    ):
        line.wait_send(buf_line, stage)
        plane.wait_send(buf_plane, stage)


def solution(mesh):
    inner_count, blk_count = mesh.shape["inner"], mesh.shape["blk"]
    pair_count = 2 if blk_count % 2 == 0 else 1
    line_count = blk_count // pair_count
    plane_count = inner_count * pair_count

    def on_device(image_emb, text_emb, logit_scale):
        rows, width = image_emb.shape
        vmem = pl.BlockSpec(memory_space=pltpu.VMEM)
        hbm = pl.BlockSpec(memory_space=pl.ANY)
        smem = pl.BlockSpec(memory_space=pltpu.SMEM)
        packed = pl.pallas_call(
            functools.partial(kernel, inner_count, line_count, pair_count),
            out_shape=pltpu.VMEM((2 * rows + 8, width), jnp.float32),
            in_specs=[smem, hbm, hbm],
            out_specs=vmem,
            scratch_shapes=[
                pltpu.VMEM((line_count, rows, width), jnp.bfloat16),
                pltpu.VMEM((plane_count, rows, width), jnp.bfloat16),
                pltpu.VMEM((line_count, 2, line_count * rows), jnp.float32),
                pltpu.VMEM((plane_count, 4, plane_count * rows), jnp.float32),
                pltpu.VMEM((plane_count, 1, 128), jnp.float32),
                pltpu.VMEM((line_count, 1, 128), jnp.float32),
                pltpu.VMEM((line_count, rows, width), jnp.bfloat16),
                pltpu.VMEM((plane_count, rows, width), jnp.bfloat16),
                pltpu.VMEM((line_count, rows, width), jnp.bfloat16),
                pltpu.VMEM((plane_count, rows, width), jnp.bfloat16),
                pltpu.VMEM((line_count, rows, width), jnp.float32),
                pltpu.VMEM((plane_count, rows, width), jnp.float32),
                pltpu.VMEM((rows, width), jnp.float32),
                pltpu.VMEM((rows, width), jnp.float32),
                pltpu.SemaphoreType.DMA((2,)),
                pltpu.SemaphoreType.DMA((4,)),
                pltpu.SemaphoreType.DMA((4,)),
                pltpu.SemaphoreType.DMA((4,)),
                pltpu.SemaphoreType.DMA((4,)),
            ],
            compiler_params=pltpu.CompilerParams(
                collective_id=0, has_side_effects=True, vmem_limit_bytes=56 * 1024 * 1024
            ),
            name="contrastive",
        )(logit_scale, image_emb, text_emb)
        return packed[2 * rows, 0:1], packed[0:rows], packed[rows : 2 * rows]

    in_specs = (P(("inner", "blk"), None), P(("inner", "blk"), None), P())
    out_specs = (P(), P(("inner", "blk"), None), P(("inner", "blk"), None))
    return jax.shard_map(
        on_device, mesh=mesh, in_specs=in_specs, out_specs=out_specs, check_vma=False
    )
```

```python
import functools

import jax
import jax.numpy as jnp
from jax import lax
from jax.experimental import pallas as pl
from jax.experimental.pallas import tpu as pltpu
from jax.sharding import PartitionSpec as P

EPSILON = 1e-06
MESH = pl.DeviceIdType.MESH


def unit_rows(values):
    inverse = lax.rsqrt(jnp.sum(values * values, axis=1, keepdims=True) + EPSILON)
    return (values * inverse, inverse)


def project(gradient, direction, inverse):
    return (gradient - direction * jnp.sum(gradient * direction, axis=1, keepdims=True)) * inverse


class Group:
    def __init__(self, me, size, device_of, order, sems):
        self.me, self.size, self.device_of, self.sems = me, size, device_of, sems
        self.order = order

    def others(self, order=None):
        order = order or self.order
        return [order(self.me, self.size, k) for k in range(1, self.size)]

    def copy(self, src, dst, stage, to):
        send_sems, recv_sems = self.sems
        return pltpu.make_async_remote_copy(
            src_ref=src,
            dst_ref=dst,
            send_sem=send_sems.at[stage],
            recv_sem=recv_sems.at[stage],
            device_id=self.device_of(to),
            device_id_type=MESH,
        )

    def whole(self, buf, stage):
        part = buf.at[pl.ds(0, self.size - 1)]
        return self.copy(part, part, stage, self.order(self.me, self.size, 1))

    def start_gather(self, buf, stage, order=None):
        mine = buf.at[self.me]
        for to in self.others(order):
            self.copy(mine, mine, stage, to).start()

    def wait_recv(self, buf, stage):
        self.whole(buf, stage).wait_recv()

    def wait_send(self, buf, stage):
        self.whole(buf, stage).wait_send()

    def start_scatter(self, parts, slots, stage, order=None):
        for to in self.others(order):
            self.copy(parts.at[to], slots.at[self.me], stage, to).start()


def ascending(me, size, k):
    return k - 1 + (k - 1 >= me).astype(jnp.int32)


def far_first(me, size, k):
    low = size - k - (size - k <= me).astype(jnp.int32)
    return jnp.where(2 * me < size, low, ascending(me, size, k))


def turned(me, size, k):
    if size & (size - 1):
        return lax.rem(me + k, size)
    out, bit = me, 1
    while bit <= k:
        if k & bit:
            out = out + bit * (1 - 2 * lax.rem(me // bit, 2))
        bit *= 2
    return out


def flipped(me, size, k):
    return turned(me, size, size - k)


def as_column(row):
    size = row.shape[1]
    shape = (size, size)
    same = lax.broadcasted_iota(jnp.int32, shape, 0) == lax.broadcasted_iota(jnp.int32, shape, 1)
    return jnp.sum(jnp.where(same, row, 0.0), axis=1, keepdims=True)


def as_row(column):
    size = column.shape[0]
    shape = (size, size)
    same = lax.broadcasted_iota(jnp.int32, shape, 0) == lax.broadcasted_iota(jnp.int32, shape, 1)
    return jnp.sum(jnp.where(same, column, 0.0), axis=0, keepdims=True)


def merge(stats):
    highest = jnp.max(stats[:, 0:1, :], axis=0)
    total = jnp.sum(stats[:, 1:2, :] * jnp.exp(stats[:, 0:1, :] - highest[None]), axis=0)
    return highest + jnp.log(total)


def flat_half(blocks):
    count, rows, width = blocks.shape
    return blocks.astype(jnp.float32).reshape(count * rows, width).astype(jnp.bfloat16)


def kernel(
    inner_count,
    line_count,
    pair_count,
    scale_ref,
    image_hbm,
    text_hbm,
    packed_ref,
    images,
    texts,
    row_stats,
    col_stats,
    row_sums,
    col_sums,
    image_parts,
    text_parts,
    image_slots,
    text_slots,
    image_own,
    text_own,
    image_ref,
    text_ref,
    input_sems,
    line_send,
    line_recv,
    plane_send,
    plane_recv,
    ready,
):
    text_in = pltpu.make_async_copy(text_hbm, text_ref, input_sems.at[0])
    image_in = pltpu.make_async_copy(image_hbm, image_ref, input_sems.at[1])
    text_in.start()
    image_in.start()
    inner, blk = lax.axis_index("inner"), lax.axis_index("blk")
    place, side = blk // pair_count, lax.rem(blk, pair_count)
    line = Group(
        place,
        line_count,
        lambda z: (inner, z * pair_count + side),
        ascending,
        (line_send, line_recv),
    )
    plane = Group(
        inner * pair_count + side,
        inner_count * pair_count,
        lambda g: (g // pair_count, place * pair_count + lax.rem(g, pair_count)),
        flipped,
        (plane_send, plane_recv),
    )
    barrier = pltpu.get_barrier_semaphore()
    pair = lambda c: (inner, place * pair_count + c)
    meets = [pair(c) for c in [lax.rem(side + k, pair_count) for k in range(1, pair_count)]]
    meets += [(inner, z * pair_count) for z in line.others()]
    meets += [
        (g, place * pair_count + pair_count - 1)
        for g in [ascending(inner, inner_count, k) for k in range(1, inner_count)]
    ]
    for to in meets:
        pl.semaphore_signal(barrier, inc=1, device_id=to, device_id_type=MESH)

    factor = scale_ref[0]
    text_in.wait()
    text_unit, text_inverse = unit_rows(text_ref[...])
    text_half = text_unit.astype(jnp.bfloat16)
    texts[plane.me] = text_half
    image_in.wait()
    image_unit, image_inverse = unit_rows(image_ref[...])
    image_half = image_unit.astype(jnp.bfloat16)
    images[line.me] = image_half
    chips = range(1, inner_count)
    near = [k for k in chips if k & (k - 1) == 0] if pair_count == 2 else list(chips)
    far = [k for k in chips if k not in near]
    chip_at = lambda k: turned(inner, inner_count, k)
    slot = lambda g, c: texts.at[g * pair_count + c]

    def text_copy(block, g, c, stage):
        return plane.copy(block, block, stage, g * pair_count + c)

    def start_texts():
        mine = slot(inner, side)
        for k in reversed(far):
            text_copy(mine, chip_at(k), side, 4).start()
        for k in near:
            for c in range(pair_count):
                text_copy(mine, chip_at(k), c, 0).start()
        if pair_count == 2:
            text_copy(mine, inner, 1 - side, 0).start()

    def some(count, stage):
        blocks = texts.at[pl.ds(0, count)]
        return plane.copy(blocks, blocks, stage, inner * pair_count + 1 - side)

    near_blocks = pair_count * len(near) + pair_count - 1

    line_met, plane_met = pair_count * (line_count - 1), pair_count * (inner_count - 1)
    if pair_count == 1:
        pl.semaphore_wait(barrier, line_met + plane_met)
        line.start_gather(images, 0, far_first)
        start_texts()
    else:
        pl.semaphore_wait(barrier, 1 + line_met + side * (plane_met - line_met))
        pl.semaphore_signal(ready, inc=1, device_id=pair(1 - side), device_id_type=MESH)

        @pl.when(side == 0)
        def _():
            line.start_gather(images, 0, far_first)
            pl.semaphore_wait(ready, 1)
            start_texts()

        @pl.when(side == 1)
        def _():
            start_texts()
            pl.semaphore_wait(ready, 1)
            line.start_gather(images, 0, far_first)

    image_back = image_half.astype(jnp.float32)
    text_back = text_half.astype(jnp.float32)
    diagonal = factor * jnp.sum(image_back * text_back)
    if far:
        some(len(far), 4).wait_recv()
        for k in far:
            text_copy(slot(chip_at(k), side), inner, 1 - side, 5).start()
    some(near_blocks, 0).wait_recv()
    line.wait_recv(images, 0)
    if far:
        some(len(far), 5).wait_recv()

    image_group = flat_half(images[...])
    text_group = flat_half(texts[...])
    image_count, text_count = image_group.shape[0], text_group.shape[0]
    logits = factor * lax.dot_general(
        image_group, text_group, (((1,), (1,)), ((), ())), preferred_element_type=jnp.float32
    )
    row_peak = jnp.max(logits, axis=1, keepdims=True)
    row_total = jnp.sum(jnp.exp(logits - row_peak), axis=1, keepdims=True)
    col_peak = jnp.max(logits, axis=0, keepdims=True)
    col_total = jnp.sum(jnp.exp(logits - col_peak), axis=0, keepdims=True)
    row_stats[line.me, 0:1, :] = as_row(row_peak)
    row_stats[line.me, 1:2, :] = as_row(row_total)
    col_stats[plane.me, 0:1, :] = col_peak
    col_stats[plane.me, 1:2, :] = col_total
    col_stats[plane.me, 2:3, :] = jnp.full((1, text_count), diagonal, jnp.float32)
    line.start_gather(row_stats, 1)
    plane.start_gather(col_stats, 1)
    line.wait_recv(row_stats, 1)
    plane.wait_recv(col_stats, 1)
    row_lse = merge(row_stats[...])
    col_lse = merge(col_stats[...])

    tile = row_sums.shape[1:]
    plane_diagonal = jnp.sum(col_stats[:, 2, 0:1])
    row_sums[plane.me] = jnp.full(tile, jnp.sum(row_lse), jnp.float32)
    col_sums[line.me] = jnp.full(tile, jnp.sum(col_lse) - 2.0 * plane_diagonal, jnp.float32)
    plane.start_gather(row_sums, 3)
    line.start_gather(col_sums, 3)

    weights = (
        0.5 * factor * (jnp.exp(logits - as_column(row_lse)) + jnp.exp(logits - col_lse))
    ).astype(jnp.bfloat16)
    image_own[...] = jnp.dot(
        weights, text_group, preferred_element_type=jnp.float32
    ).reshape(image_parts.shape)
    image_parts[...] = image_own[...].astype(jnp.bfloat16)
    line.start_scatter(image_parts, image_slots, 2)
    text_own[...] = lax.dot_general(
        weights, image_group, (((0,), (0,)), ((), ())), preferred_element_type=jnp.float32
    ).reshape(text_parts.shape)
    text_parts[...] = text_own[...].astype(jnp.bfloat16)
    plane.start_scatter(text_parts, text_slots, 2, ascending)

    rows = image_ref.shape[0]
    plane.wait_recv(text_slots, 2)
    text_sum = text_own[plane.me]
    for other in plane.others():
        text_sum = text_sum + text_slots[other].astype(jnp.float32)
    packed_ref[pl.ds(rows, rows)] = project(text_sum - factor * image_back, text_unit, text_inverse)
    line.wait_recv(image_slots, 2)
    image_sum = image_own[line.me]
    for other in line.others():
        image_sum = image_sum + image_slots[other].astype(jnp.float32)
    packed_ref[pl.ds(0, rows)] = project(image_sum - factor * text_back, image_unit, image_inverse)

    plane.wait_recv(row_sums, 3)
    line.wait_recv(col_sums, 3)
    examples = 2.0 * line.size * plane.size * rows
    whole = jnp.sum(row_sums[...], axis=0)[0:1, 0:1] + jnp.sum(col_sums[...], axis=0)[0:1, 0:1]
    packed_ref[pl.ds(2 * rows, 8)] = jnp.broadcast_to(whole / examples, (8, packed_ref.shape[1]))
    line.wait_send(images, 0)
    some(near_blocks, 0).wait_send()
    if far:
        some(len(far), 4).wait_send()
        some(len(far), 5).wait_send()
    for buf_line, buf_plane, stage in (
        (row_stats, col_stats, 1),
        (image_parts, text_parts, 2),
        (col_sums, row_sums, 3),
    ):
        line.wait_send(buf_line, stage)
        plane.wait_send(buf_plane, stage)


def solution(mesh):
    inner_count, blk_count = mesh.shape["inner"], mesh.shape["blk"]
    pair_count = 2 if blk_count % 2 == 0 else 1
    line_count = blk_count // pair_count
    plane_count = inner_count * pair_count

    def on_device(image_emb, text_emb, logit_scale):
        rows, width = image_emb.shape
        vmem = pl.BlockSpec(memory_space=pltpu.VMEM)
        hbm = pl.BlockSpec(memory_space=pl.ANY)
        smem = pl.BlockSpec(memory_space=pltpu.SMEM)
        packed = pl.pallas_call(
            functools.partial(kernel, inner_count, line_count, pair_count),
            out_shape=pltpu.VMEM((2 * rows + 8, width), jnp.float32),
            in_specs=[smem, hbm, hbm],
            out_specs=vmem,
            scratch_shapes=[
                pltpu.VMEM((line_count, rows, width), jnp.bfloat16),
                pltpu.VMEM((plane_count, rows, width), jnp.bfloat16),
                pltpu.VMEM((line_count, 2, line_count * rows), jnp.float32),
                pltpu.VMEM((plane_count, 4, plane_count * rows), jnp.float32),
                pltpu.VMEM((plane_count, 1, 128), jnp.float32),
                pltpu.VMEM((line_count, 1, 128), jnp.float32),
                pltpu.VMEM((line_count, rows, width), jnp.bfloat16),
                pltpu.VMEM((plane_count, rows, width), jnp.bfloat16),
                pltpu.VMEM((line_count, rows, width), jnp.bfloat16),
                pltpu.VMEM((plane_count, rows, width), jnp.bfloat16),
                pltpu.VMEM((line_count, rows, width), jnp.float32),
                pltpu.VMEM((plane_count, rows, width), jnp.float32),
                pltpu.VMEM((rows, width), jnp.float32),
                pltpu.VMEM((rows, width), jnp.float32),
                pltpu.SemaphoreType.DMA((2,)),
                pltpu.SemaphoreType.DMA((4,)),
                pltpu.SemaphoreType.DMA((4,)),
                pltpu.SemaphoreType.DMA((6,)),
                pltpu.SemaphoreType.DMA((6,)),
                pltpu.SemaphoreType.REGULAR,
            ],
            compiler_params=pltpu.CompilerParams(
                collective_id=0, has_side_effects=True, vmem_limit_bytes=56 * 1024 * 1024
            ),
            name="contrastive",
        )(logit_scale, image_emb, text_emb)
        return packed[2 * rows, 0:1], packed[0:rows], packed[rows : 2 * rows]

    in_specs = (P(("inner", "blk"), None), P(("inner", "blk"), None), P())
    out_specs = (P(), P(("inner", "blk"), None), P(("inner", "blk"), None))
    return jax.shard_map(
        on_device, mesh=mesh, in_specs=in_specs, out_specs=out_specs, check_vma=False
    )
```

```python
import functools

import jax
import jax.numpy as jnp
from jax import lax
from jax.experimental import pallas as pl
from jax.experimental.pallas import tpu as pltpu
from jax.sharding import PartitionSpec as P

EPSILON = 1e-06
MESH = pl.DeviceIdType.MESH


def unit_rows(values):
    inverse = lax.rsqrt(jnp.sum(values * values, axis=1, keepdims=True) + EPSILON)
    return (values * inverse, inverse)


def project(gradient, direction, inverse):
    return (gradient - direction * jnp.sum(gradient * direction, axis=1, keepdims=True)) * inverse


class Group:
    def __init__(self, me, size, device_of, order, sems):
        self.me, self.size, self.device_of, self.sems = me, size, device_of, sems
        self.order = order

    def others(self, order=None):
        order = order or self.order
        return [order(self.me, self.size, k) for k in range(1, self.size)]

    def copy(self, src, dst, stage, to):
        send_sems, recv_sems = self.sems
        return pltpu.make_async_remote_copy(
            src_ref=src,
            dst_ref=dst,
            send_sem=send_sems.at[stage],
            recv_sem=recv_sems.at[stage],
            device_id=self.device_of(to),
            device_id_type=MESH,
        )

    def whole(self, buf, stage):
        part = buf.at[pl.ds(0, self.size - 1)]
        return self.copy(part, part, stage, self.order(self.me, self.size, 1))

    def start_gather(self, buf, stage, order=None):
        mine = buf.at[self.me]
        for to in self.others(order):
            self.copy(mine, mine, stage, to).start()

    def wait_recv(self, buf, stage):
        self.whole(buf, stage).wait_recv()

    def wait_send(self, buf, stage):
        self.whole(buf, stage).wait_send()

    def start_scatter(self, parts, slots, stage, order=None, part=slice(None)):
        for to in self.others(order)[part]:
            self.copy(parts.at[to], slots.at[self.me], stage, to).start()


def ascending(me, size, k):
    return k - 1 + (k - 1 >= me).astype(jnp.int32)


def far_first(me, size, k):
    low = size - k - (size - k <= me).astype(jnp.int32)
    return jnp.where(2 * me < size, low, ascending(me, size, k))


def turned(me, size, k):
    if size & (size - 1):
        return lax.rem(me + k, size)
    out, bit = me, 1
    while bit <= k:
        if k & bit:
            out = out + bit * (1 - 2 * lax.rem(me // bit, 2))
        bit *= 2
    return out


def flipped(me, size, k):
    return turned(me, size, size - k)


def as_column(row):
    size = row.shape[1]
    shape = (size, size)
    same = lax.broadcasted_iota(jnp.int32, shape, 0) == lax.broadcasted_iota(jnp.int32, shape, 1)
    return jnp.sum(jnp.where(same, row, 0.0), axis=1, keepdims=True)


def as_row(column):
    size = column.shape[0]
    shape = (size, size)
    same = lax.broadcasted_iota(jnp.int32, shape, 0) == lax.broadcasted_iota(jnp.int32, shape, 1)
    return jnp.sum(jnp.where(same, column, 0.0), axis=0, keepdims=True)


def merge(stats):
    highest = jnp.max(stats[:, 0:1, :], axis=0)
    total = jnp.sum(stats[:, 1:2, :] * jnp.exp(stats[:, 0:1, :] - highest[None]), axis=0)
    return highest + jnp.log(total)


def flat_half(blocks):
    count, rows, width = blocks.shape
    return blocks.astype(jnp.float32).reshape(count * rows, width).astype(jnp.bfloat16)


def kernel(
    inner_count,
    line_count,
    pair_count,
    scale_ref,
    image_hbm,
    text_hbm,
    loss_ref,
    image_grad_ref,
    text_grad_ref,
    images,
    texts,
    row_stats,
    col_stats,
    row_sums,
    col_sums,
    image_parts,
    text_parts,
    image_slots,
    text_slots,
    image_own,
    text_own,
    image_ref,
    text_ref,
    input_sems,
    line_send,
    line_recv,
    plane_send,
    plane_recv,
    ready,
):
    text_in = pltpu.make_async_copy(text_hbm, text_ref, input_sems.at[0])
    image_in = pltpu.make_async_copy(image_hbm, image_ref, input_sems.at[1])
    text_in.start()
    image_in.start()
    inner, blk = lax.axis_index("inner"), lax.axis_index("blk")
    place, side = blk // pair_count, lax.rem(blk, pair_count)
    line = Group(
        place,
        line_count,
        lambda z: (inner, z * pair_count + side),
        ascending,
        (line_send, line_recv),
    )
    plane = Group(
        inner * pair_count + side,
        inner_count * pair_count,
        lambda g: (g // pair_count, place * pair_count + lax.rem(g, pair_count)),
        flipped,
        (plane_send, plane_recv),
    )
    barrier = pltpu.get_barrier_semaphore()
    pair = lambda c: (inner, place * pair_count + c)
    meets = [pair(c) for c in [lax.rem(side + k, pair_count) for k in range(1, pair_count)]]
    meets += [(inner, z * pair_count) for z in line.others()]
    meets += [
        (g, place * pair_count + pair_count - 1)
        for g in [ascending(inner, inner_count, k) for k in range(1, inner_count)]
    ]
    for to in meets:
        pl.semaphore_signal(barrier, inc=1, device_id=to, device_id_type=MESH)

    factor = scale_ref[0]
    text_in.wait()
    text_unit, text_inverse = unit_rows(text_ref[...])
    text_half = text_unit.astype(jnp.bfloat16)
    texts[plane.me] = text_half
    image_in.wait()
    image_unit, image_inverse = unit_rows(image_ref[...])
    image_half = image_unit.astype(jnp.bfloat16)
    images[line.me] = image_half
    chips = range(1, inner_count)
    near = [k for k in chips if k & (k - 1) == 0] if pair_count == 2 else list(chips)
    far = [k for k in chips if k not in near]
    chip_at = lambda k: turned(inner, inner_count, k)
    slot = lambda g, c: texts.at[g * pair_count + c]

    def text_copy(block, g, c, stage):
        return plane.copy(block, block, stage, g * pair_count + c)

    def start_texts():
        mine = slot(inner, side)
        for k in reversed(far):
            text_copy(mine, chip_at(k), side, 4).start()
        for k in near:
            for c in range(pair_count):
                text_copy(mine, chip_at(k), c, 0).start()
        if pair_count == 2:
            text_copy(mine, inner, 1 - side, 0).start()

    def some(count, stage):
        blocks = texts.at[pl.ds(0, count)]
        return plane.copy(blocks, blocks, stage, inner * pair_count + 1 - side)

    near_blocks = pair_count * len(near) + pair_count - 1

    line_met, plane_met = pair_count * (line_count - 1), pair_count * (inner_count - 1)
    if pair_count == 1:
        pl.semaphore_wait(barrier, line_met + plane_met)
        line.start_gather(images, 0, far_first)
        start_texts()
    else:
        pl.semaphore_wait(barrier, 1 + line_met + side * (plane_met - line_met))
        pl.semaphore_signal(ready, inc=1, device_id=pair(1 - side), device_id_type=MESH)

        @pl.when(side == 0)
        def _():
            line.start_gather(images, 0, far_first)
            pl.semaphore_wait(ready, 1)
            start_texts()

        @pl.when(side == 1)
        def _():
            start_texts()
            pl.semaphore_wait(ready, 1)
            line.start_gather(images, 0, far_first)

    image_back = image_half.astype(jnp.float32)
    text_back = text_half.astype(jnp.float32)
    diagonal = factor * jnp.sum(image_back * text_back)
    if far:
        some(len(far), 4).wait_recv()
        for k in far:
            text_copy(slot(chip_at(k), side), inner, 1 - side, 5).start()
    some(near_blocks, 0).wait_recv()
    line.wait_recv(images, 0)
    if far:
        some(len(far), 5).wait_recv()

    image_group = flat_half(images[...])
    text_group = flat_half(texts[...])
    image_count, text_count = image_group.shape[0], text_group.shape[0]
    logits = factor * lax.dot_general(
        image_group, text_group, (((1,), (1,)), ((), ())), preferred_element_type=jnp.float32
    )
    row_peak = jnp.max(logits, axis=1, keepdims=True)
    row_total = jnp.sum(jnp.exp(logits - row_peak), axis=1, keepdims=True)
    col_peak = jnp.max(logits, axis=0, keepdims=True)
    col_total = jnp.sum(jnp.exp(logits - col_peak), axis=0, keepdims=True)
    row_stats[line.me, 0:1, :] = as_row(row_peak)
    row_stats[line.me, 1:2, :] = as_row(row_total)
    col_stats[plane.me, 0:1, :] = col_peak
    col_stats[plane.me, 1:2, :] = col_total
    col_stats[plane.me, 2:3, :] = jnp.full((1, text_count), diagonal, jnp.float32)
    line.start_gather(row_stats, 1)
    plane.start_gather(col_stats, 1)
    line.wait_recv(row_stats, 1)
    plane.wait_recv(col_stats, 1)
    row_lse = merge(row_stats[...])
    col_lse = merge(col_stats[...])

    weights = (
        0.5 * factor * (jnp.exp(logits - as_column(row_lse)) + jnp.exp(logits - col_lse))
    ).astype(jnp.bfloat16)
    image_own[...] = jnp.dot(
        weights, text_group, preferred_element_type=jnp.float32
    ).reshape(image_parts.shape)
    image_parts[...] = image_own[...].astype(jnp.bfloat16)
    line.start_scatter(image_parts, image_slots, 2, part=slice(0, 1))
    text_own[...] = lax.dot_general(
        weights, image_group, (((0,), (0,)), ((), ())), preferred_element_type=jnp.float32
    ).reshape(text_parts.shape)
    text_parts[...] = text_own[...].astype(jnp.bfloat16)
    plane.start_scatter(text_parts, text_slots, 2, ascending, slice(0, pair_count))
    tile = row_sums.shape[1:]
    plane_diagonal = jnp.sum(col_stats[:, 2, 0:1])
    row_sums[plane.me] = jnp.full(tile, jnp.sum(row_lse), jnp.float32)
    col_sums[line.me] = jnp.full(tile, jnp.sum(col_lse) - 2.0 * plane_diagonal, jnp.float32)
    plane.start_gather(row_sums, 3)
    line.start_gather(col_sums, 3)
    line.start_scatter(image_parts, image_slots, 2, part=slice(1, None))
    plane.start_scatter(text_parts, text_slots, 2, ascending, slice(pair_count, None))

    rows = image_ref.shape[0]
    plane.wait_recv(text_slots, 2)
    text_sum = text_own[plane.me]
    for other in plane.others():
        text_sum = text_sum + text_slots[other].astype(jnp.float32)
    text_grad_ref[...] = project(text_sum - factor * image_back, text_unit, text_inverse)
    line.wait_recv(image_slots, 2)
    image_sum = image_own[line.me]
    for other in line.others():
        image_sum = image_sum + image_slots[other].astype(jnp.float32)
    image_grad_ref[...] = project(image_sum - factor * text_back, image_unit, image_inverse)

    plane.wait_recv(row_sums, 3)
    line.wait_recv(col_sums, 3)
    examples = 2.0 * line.size * plane.size * rows
    whole = jnp.sum(row_sums[...], axis=0)[0:1, 0:1] + jnp.sum(col_sums[...], axis=0)[0:1, 0:1]
    loss_ref[...] = jnp.broadcast_to(whole / examples, loss_ref.shape)
    line.wait_send(images, 0)
    some(near_blocks, 0).wait_send()
    if far:
        some(len(far), 4).wait_send()
        some(len(far), 5).wait_send()
    for buf_line, buf_plane, stage in (
        (row_stats, col_stats, 1),
        (image_parts, text_parts, 2),
        (col_sums, row_sums, 3),
    ):
        line.wait_send(buf_line, stage)
        plane.wait_send(buf_plane, stage)


def store(loss, image_grad, text_grad, loss_hbm, image_hbm, text_hbm, sems):
    pairs = ((image_grad, image_hbm), (text_grad, text_hbm), (loss, loss_hbm))
    copies = [pltpu.make_async_copy(*pair, sems.at[k]) for k, pair in enumerate(pairs)]
    for copy in copies:
        copy.start()
    for copy in copies:
        copy.wait()


def solution(mesh):
    inner_count, blk_count = mesh.shape["inner"], mesh.shape["blk"]
    pair_count = 2 if blk_count % 2 == 0 else 1
    line_count = blk_count // pair_count
    plane_count = inner_count * pair_count

    def on_device(image_emb, text_emb, logit_scale):
        rows, width = image_emb.shape
        vmem = pl.BlockSpec(memory_space=pltpu.VMEM)
        hbm = pl.BlockSpec(memory_space=pl.ANY)
        smem = pl.BlockSpec(memory_space=pltpu.SMEM)
        near = pltpu.VMEM((rows, width), jnp.float32)
        results = pl.pallas_call(
            functools.partial(kernel, inner_count, line_count, pair_count),
            out_shape=(pltpu.VMEM((1, 128), jnp.float32), near, near),
            in_specs=[smem, hbm, hbm],
            out_specs=(vmem, vmem, vmem),
            scratch_shapes=[
                pltpu.VMEM((line_count, rows, width), jnp.bfloat16),
                pltpu.VMEM((plane_count, rows, width), jnp.bfloat16),
                pltpu.VMEM((line_count, 2, line_count * rows), jnp.float32),
                pltpu.VMEM((plane_count, 4, plane_count * rows), jnp.float32),
                pltpu.VMEM((plane_count, 1, 128), jnp.float32),
                pltpu.VMEM((line_count, 1, 128), jnp.float32),
                pltpu.VMEM((line_count, rows, width), jnp.bfloat16),
                pltpu.VMEM((plane_count, rows, width), jnp.bfloat16),
                pltpu.VMEM((line_count, rows, width), jnp.bfloat16),
                pltpu.VMEM((plane_count, rows, width), jnp.bfloat16),
                pltpu.VMEM((line_count, rows, width), jnp.float32),
                pltpu.VMEM((plane_count, rows, width), jnp.float32),
                pltpu.VMEM((rows, width), jnp.float32),
                pltpu.VMEM((rows, width), jnp.float32),
                pltpu.SemaphoreType.DMA((2,)),
                pltpu.SemaphoreType.DMA((4,)),
                pltpu.SemaphoreType.DMA((4,)),
                pltpu.SemaphoreType.DMA((6,)),
                pltpu.SemaphoreType.DMA((6,)),
                pltpu.SemaphoreType.REGULAR,
            ],
            compiler_params=pltpu.CompilerParams(
                collective_id=0, has_side_effects=True, vmem_limit_bytes=56 * 1024 * 1024
            ),
            name="contrastive",
        )(logit_scale, image_emb, text_emb)
        far = jax.ShapeDtypeStruct((rows, width), jnp.float32)
        loss, image_grad, text_grad = pl.pallas_call(
            store,
            out_shape=(jax.ShapeDtypeStruct((1, 128), jnp.float32), far, far),
            in_specs=[vmem, vmem, vmem],
            out_specs=(hbm, hbm, hbm),
            scratch_shapes=[pltpu.SemaphoreType.DMA((3,))],
            compiler_params=pltpu.CompilerParams(vmem_limit_bytes=16 * 1024 * 1024),
            name="store",
        )(*results)
        return loss.reshape(128)[0:1], image_grad, text_grad

    in_specs = (P(("inner", "blk"), None), P(("inner", "blk"), None), P())
    out_specs = (P(), P(("inner", "blk"), None), P(("inner", "blk"), None))
    return jax.shard_map(
        on_device, mesh=mesh, in_specs=in_specs, out_specs=out_specs, check_vma=False
    )
```

```python
import functools

import jax
import jax.numpy as jnp
from jax import lax
from jax.experimental import pallas as pl
from jax.experimental.pallas import tpu as pltpu
from jax.sharding import PartitionSpec as P

EPSILON = 1e-06
MESH = pl.DeviceIdType.MESH


def unit_rows(values):
    inverse = lax.rsqrt(jnp.sum(values * values, axis=1, keepdims=True) + EPSILON)
    return (values * inverse, inverse)


def project(gradient, direction, inverse):
    return (gradient - direction * jnp.sum(gradient * direction, axis=1, keepdims=True)) * inverse


class Group:
    def __init__(self, me, size, device_of, order, sems):
        self.me, self.size, self.device_of, self.sems = me, size, device_of, sems
        self.order = order

    def others(self, order=None):
        order = order or self.order
        return [order(self.me, self.size, k) for k in range(1, self.size)]

    def copy(self, src, dst, stage, to, later=None):
        send_sems, recv_sems = self.sems
        return pltpu.make_async_remote_copy(
            src_ref=src,
            dst_ref=dst,
            send_sem=send_sems.at[stage if later is None else later],
            recv_sem=recv_sems.at[stage],
            device_id=self.device_of(to),
            device_id_type=MESH,
        )

    def whole(self, buf, stage):
        part = buf.at[pl.ds(0, self.size - 1)]
        return self.copy(part, part, stage, self.order(self.me, self.size, 1))

    def start_gather(self, buf, stage, order=None):
        mine = buf.at[self.me]
        for to in self.others(order):
            self.copy(mine, mine, stage, to).start()

    def wait_recv(self, buf, stage):
        self.whole(buf, stage).wait_recv()

    def wait_send(self, buf, stage):
        self.whole(buf, stage).wait_send()

    def wait_some(self, buf, stage, count):
        part = buf.at[pl.ds(0, count)]
        self.copy(part, part, stage, self.order(self.me, self.size, 1)).wait_send()

    def start_scatter(self, parts, slots, stage, order=None, part=slice(None), later=None):
        for to in self.others(order)[part]:
            self.copy(parts.at[to], slots.at[self.me], stage, to, later).start()


def ascending(me, size, k):
    return k - 1 + (k - 1 >= me).astype(jnp.int32)


def far_first(me, size, k):
    low = size - k - (size - k <= me).astype(jnp.int32)
    return jnp.where(2 * me < size, low, ascending(me, size, k))


def turned(me, size, k):
    if size & (size - 1):
        return lax.rem(me + k, size)
    out, bit = me, 1
    while bit <= k:
        if k & bit:
            out = out + bit * (1 - 2 * lax.rem(me // bit, 2))
        bit *= 2
    return out


def flipped(me, size, k):
    return turned(me, size, size - k)


def as_column(row):
    size = row.shape[1]
    shape = (size, size)
    same = lax.broadcasted_iota(jnp.int32, shape, 0) == lax.broadcasted_iota(jnp.int32, shape, 1)
    return jnp.sum(jnp.where(same, row, 0.0), axis=1, keepdims=True)


def as_row(column):
    size = column.shape[0]
    shape = (size, size)
    same = lax.broadcasted_iota(jnp.int32, shape, 0) == lax.broadcasted_iota(jnp.int32, shape, 1)
    return jnp.sum(jnp.where(same, column, 0.0), axis=0, keepdims=True)


def merge(stats):
    highest = jnp.max(stats[:, 0:1, :], axis=0)
    total = jnp.sum(stats[:, 1:2, :] * jnp.exp(stats[:, 0:1, :] - highest[None]), axis=0)
    return highest + jnp.log(total)


def flat_half(blocks):
    count, rows, width = blocks.shape
    return blocks.astype(jnp.float32).reshape(count * rows, width).astype(jnp.bfloat16)


def kernel(
    inner_count,
    line_count,
    pair_count,
    scale_ref,
    image_hbm,
    text_hbm,
    loss_ref,
    image_grad_ref,
    text_grad_ref,
    images,
    texts,
    row_stats,
    col_stats,
    row_sums,
    col_sums,
    image_parts,
    text_parts,
    image_slots,
    text_slots,
    image_own,
    text_own,
    image_ref,
    text_ref,
    input_sems,
    line_send,
    line_recv,
    plane_send,
    plane_recv,
):
    text_in = pltpu.make_async_copy(text_hbm, text_ref, input_sems.at[0])
    image_in = pltpu.make_async_copy(image_hbm, image_ref, input_sems.at[1])
    text_in.start()
    image_in.start()
    inner, blk = lax.axis_index("inner"), lax.axis_index("blk")
    place, side = blk // pair_count, lax.rem(blk, pair_count)
    line = Group(
        place,
        line_count,
        lambda z: (inner, z * pair_count + side),
        ascending,
        (line_send, line_recv),
    )
    plane = Group(
        inner * pair_count + side,
        inner_count * pair_count,
        lambda g: (g // pair_count, place * pair_count + lax.rem(g, pair_count)),
        flipped,
        (plane_send, plane_recv),
    )
    barrier = pltpu.get_barrier_semaphore()
    meets = [group.device_of(to) for group in (plane, line) for to in group.others()]
    for to in meets:
        pl.semaphore_signal(barrier, inc=1, device_id=to, device_id_type=MESH)

    factor = scale_ref[0]
    text_in.wait()
    text_unit, text_inverse = unit_rows(text_ref[...])
    text_half = text_unit.astype(jnp.bfloat16)
    texts[plane.me] = text_half
    image_in.wait()
    image_unit, image_inverse = unit_rows(image_ref[...])
    image_half = image_unit.astype(jnp.bfloat16)
    images[line.me] = image_half
    chips = range(1, inner_count)
    near = [k for k in chips if k & (k - 1) == 0] if pair_count == 2 else list(chips)
    far = [k for k in chips if k not in near]
    chip_at = lambda k: turned(inner, inner_count, k)
    slot = lambda g, c: texts.at[g * pair_count + c]

    def text_copy(block, g, c, stage):
        return plane.copy(block, block, stage, g * pair_count + c)

    def start_texts():
        mine = slot(inner, side)
        for k in reversed(far):
            text_copy(mine, chip_at(k), side, 4).start()
        for k in near:
            for c in range(pair_count):
                text_copy(mine, chip_at(k), c, 0).start()
        if pair_count == 2:
            text_copy(mine, inner, 1 - side, 0).start()

    def some(count, stage):
        blocks = texts.at[pl.ds(0, count)]
        return plane.copy(blocks, blocks, stage, inner * pair_count + 1 - side)

    near_blocks = pair_count * len(near) + pair_count - 1

    pl.semaphore_wait(barrier, plane.size + line.size - 2)
    line.start_gather(images, 0, far_first)
    start_texts()
    image_back = image_half.astype(jnp.float32)
    text_back = text_half.astype(jnp.float32)
    diagonal = factor * jnp.sum(image_back * text_back)
    if far:
        some(len(far), 4).wait_recv()
        for k in far:
            text_copy(slot(chip_at(k), side), inner, 1 - side, 5).start()
    some(near_blocks, 0).wait_recv()
    line.wait_recv(images, 0)
    if far:
        some(len(far), 5).wait_recv()

    image_group = flat_half(images[...])
    text_group = flat_half(texts[...])
    image_count, text_count = image_group.shape[0], text_group.shape[0]
    logits = factor * lax.dot_general(
        image_group, text_group, (((1,), (1,)), ((), ())), preferred_element_type=jnp.float32
    )
    row_peak = jnp.max(logits, axis=1, keepdims=True)
    row_total = jnp.sum(jnp.exp(logits - row_peak), axis=1, keepdims=True)
    col_peak = jnp.max(logits, axis=0, keepdims=True)
    col_total = jnp.sum(jnp.exp(logits - col_peak), axis=0, keepdims=True)
    row_stats[line.me, 0:1, :] = as_row(row_peak)
    row_stats[line.me, 1:2, :] = as_row(row_total)
    col_stats[plane.me, 0:1, :] = col_peak
    col_stats[plane.me, 1:2, :] = col_total
    col_stats[plane.me, 2:3, :] = jnp.full((1, text_count), diagonal, jnp.float32)
    line.start_gather(row_stats, 1)
    plane.start_gather(col_stats, 1)
    line.wait_recv(row_stats, 1)
    plane.wait_recv(col_stats, 1)
    row_lse = merge(row_stats[...])
    col_lse = merge(col_stats[...])

    weights = (
        0.5 * factor * (jnp.exp(logits - as_column(row_lse)) + jnp.exp(logits - col_lse))
    ).astype(jnp.bfloat16)
    image_own[...] = jnp.dot(
        weights, text_group, preferred_element_type=jnp.float32
    ).reshape(image_parts.shape)
    image_parts[...] = image_own[...].astype(jnp.bfloat16)
    line.start_scatter(image_parts, image_slots, 2, part=slice(0, 1))
    text_own[...] = lax.dot_general(
        weights, image_group, (((0,), (0,)), ((), ())), preferred_element_type=jnp.float32
    ).reshape(text_parts.shape)
    text_parts[...] = text_own[...].astype(jnp.bfloat16)
    plane.start_scatter(text_parts, text_slots, 2, ascending, slice(0, pair_count))
    tile = row_sums.shape[1:]
    plane_diagonal = jnp.sum(col_stats[:, 2, 0:1])
    row_sums[plane.me] = jnp.full(tile, jnp.sum(row_lse), jnp.float32)
    col_sums[line.me] = jnp.full(tile, jnp.sum(col_lse) - 2.0 * plane_diagonal, jnp.float32)
    plane.start_gather(row_sums, 3)
    line.start_gather(col_sums, 3)
    line.wait_some(image_parts, 2, 1)
    line.start_scatter(image_parts, image_slots, 2, part=slice(1, None), later=4)
    plane.start_scatter(text_parts, text_slots, 2, ascending, slice(pair_count, None), 6)

    rows = image_ref.shape[0]
    plane.wait_recv(text_slots, 2)
    text_sum = text_own[plane.me]
    for other in plane.others():
        text_sum = text_sum + text_slots[other].astype(jnp.float32)
    text_grad_ref[...] = project(text_sum - factor * image_back, text_unit, text_inverse)
    line.wait_recv(image_slots, 2)
    image_sum = image_own[line.me]
    for other in line.others():
        image_sum = image_sum + image_slots[other].astype(jnp.float32)
    image_grad_ref[...] = project(image_sum - factor * text_back, image_unit, image_inverse)

    plane.wait_recv(row_sums, 3)
    line.wait_recv(col_sums, 3)
    examples = 2.0 * line.size * plane.size * rows
    whole = jnp.sum(row_sums[...], axis=0)[0:1, 0:1] + jnp.sum(col_sums[...], axis=0)[0:1, 0:1]
    loss_ref[...] = jnp.broadcast_to(whole / examples, loss_ref.shape)
    plane.wait_some(text_parts, 2, pair_count)
    line.wait_some(image_parts, 4, line_count - 2)
    plane.wait_some(text_parts, 6, plane.size - 1 - pair_count)
    line.wait_send(images, 0)
    some(near_blocks, 0).wait_send()
    if far:
        some(len(far), 4).wait_send()
        some(len(far), 5).wait_send()
    for buf_line, buf_plane, stage in (
        (row_stats, col_stats, 1),
        (col_sums, row_sums, 3),
    ):
        line.wait_send(buf_line, stage)
        plane.wait_send(buf_plane, stage)


def store(loss, image_grad, text_grad, loss_hbm, image_hbm, text_hbm, sems):
    pairs = ((image_grad, image_hbm), (text_grad, text_hbm), (loss, loss_hbm))
    copies = [pltpu.make_async_copy(*pair, sems.at[k]) for k, pair in enumerate(pairs)]
    for copy in copies:
        copy.start()
    for copy in copies:
        copy.wait()


def solution(mesh):
    inner_count, blk_count = mesh.shape["inner"], mesh.shape["blk"]
    pair_count = 2 if blk_count % 2 == 0 else 1
    line_count = blk_count // pair_count
    plane_count = inner_count * pair_count

    def on_device(image_emb, text_emb, logit_scale):
        rows, width = image_emb.shape
        vmem = pl.BlockSpec(memory_space=pltpu.VMEM)
        hbm = pl.BlockSpec(memory_space=pl.ANY)
        smem = pl.BlockSpec(memory_space=pltpu.SMEM)
        near = pltpu.VMEM((rows, width), jnp.float32)
        results = pl.pallas_call(
            functools.partial(kernel, inner_count, line_count, pair_count),
            out_shape=(pltpu.VMEM((1, 128), jnp.float32), near, near),
            in_specs=[smem, hbm, hbm],
            out_specs=(vmem, vmem, vmem),
            scratch_shapes=[
                pltpu.VMEM((line_count, rows, width), jnp.bfloat16),
                pltpu.VMEM((plane_count, rows, width), jnp.bfloat16),
                pltpu.VMEM((line_count, 2, line_count * rows), jnp.float32),
                pltpu.VMEM((plane_count, 4, plane_count * rows), jnp.float32),
                pltpu.VMEM((plane_count, 1, 128), jnp.float32),
                pltpu.VMEM((line_count, 1, 128), jnp.float32),
                pltpu.VMEM((line_count, rows, width), jnp.bfloat16),
                pltpu.VMEM((plane_count, rows, width), jnp.bfloat16),
                pltpu.VMEM((line_count, rows, width), jnp.bfloat16),
                pltpu.VMEM((plane_count, rows, width), jnp.bfloat16),
                pltpu.VMEM((line_count, rows, width), jnp.float32),
                pltpu.VMEM((plane_count, rows, width), jnp.float32),
                pltpu.VMEM((rows, width), jnp.float32),
                pltpu.VMEM((rows, width), jnp.float32),
                pltpu.SemaphoreType.DMA((2,)),
                pltpu.SemaphoreType.DMA((5,)),
                pltpu.SemaphoreType.DMA((5,)),
                pltpu.SemaphoreType.DMA((7,)),
                pltpu.SemaphoreType.DMA((7,)),
            ],
            compiler_params=pltpu.CompilerParams(
                collective_id=0, has_side_effects=True, vmem_limit_bytes=56 * 1024 * 1024
            ),
            name="contrastive",
        )(logit_scale, image_emb, text_emb)
        far = jax.ShapeDtypeStruct((rows, width), jnp.float32)
        loss, image_grad, text_grad = pl.pallas_call(
            store,
            out_shape=(jax.ShapeDtypeStruct((1, 128), jnp.float32), far, far),
            in_specs=[vmem, vmem, vmem],
            out_specs=(hbm, hbm, hbm),
            scratch_shapes=[pltpu.SemaphoreType.DMA((3,))],
            compiler_params=pltpu.CompilerParams(vmem_limit_bytes=16 * 1024 * 1024),
            name="store",
        )(*results)
        return loss.reshape(128)[0:1], image_grad, text_grad

    in_specs = (P(("inner", "blk"), None), P(("inner", "blk"), None), P())
    out_specs = (P(), P(("inner", "blk"), None), P(("inner", "blk"), None))
    return jax.shard_map(
        on_device, mesh=mesh, in_specs=in_specs, out_specs=out_specs, check_vma=False
    )
```

```python
import functools

import jax
import jax.numpy as jnp
from jax import lax
from jax.experimental import pallas as pl
from jax.experimental.pallas import tpu as pltpu
from jax.sharding import PartitionSpec as P

EPSILON = 1e-06
MESH = pl.DeviceIdType.MESH


def unit_rows(values):
    inverse = lax.rsqrt(jnp.sum(values * values, axis=1, keepdims=True) + EPSILON)
    return (values * inverse, inverse)


def project(gradient, direction, inverse):
    return (gradient - direction * jnp.sum(gradient * direction, axis=1, keepdims=True)) * inverse


class Group:
    def __init__(self, me, size, device_of, order, sems):
        self.me, self.size, self.device_of, self.sems = me, size, device_of, sems
        self.order = order

    def others(self, order=None):
        order = order or self.order
        return [order(self.me, self.size, k) for k in range(1, self.size)]

    def copy(self, src, dst, stage, to, later=None):
        send_sems, recv_sems = self.sems
        return pltpu.make_async_remote_copy(
            src_ref=src,
            dst_ref=dst,
            send_sem=send_sems.at[stage if later is None else later],
            recv_sem=recv_sems.at[stage],
            device_id=self.device_of(to),
            device_id_type=MESH,
        )

    def whole(self, buf, stage):
        part = buf.at[pl.ds(0, self.size - 1)]
        return self.copy(part, part, stage, self.order(self.me, self.size, 1))

    def start_gather(self, buf, stage, order=None):
        mine = buf.at[self.me]
        for to in self.others(order):
            self.copy(mine, mine, stage, to).start()

    def wait_recv(self, buf, stage):
        self.whole(buf, stage).wait_recv()

    def wait_send(self, buf, stage):
        self.whole(buf, stage).wait_send()

    def wait_some(self, buf, stage, count):
        part = buf.at[pl.ds(0, count)]
        self.copy(part, part, stage, self.order(self.me, self.size, 1)).wait_send()

    def start_scatter(self, parts, slots, stage, order=None, part=slice(None), later=None):
        for to in self.others(order)[part]:
            self.copy(parts.at[to], slots.at[self.me], stage, to, later).start()


def ascending(me, size, k):
    return k - 1 + (k - 1 >= me).astype(jnp.int32)


def far_first(me, size, k):
    low = size - k - (size - k <= me).astype(jnp.int32)
    return jnp.where(2 * me < size, low, ascending(me, size, k))


def turned(me, size, k):
    if size & (size - 1):
        return lax.rem(me + k, size)
    out, bit = me, 1
    while bit <= k:
        if k & bit:
            out = out + bit * (1 - 2 * lax.rem(me // bit, 2))
        bit *= 2
    return out


def flipped(me, size, k):
    return turned(me, size, size - k)


def as_column(row):
    size = row.shape[1]
    shape = (size, size)
    same = lax.broadcasted_iota(jnp.int32, shape, 0) == lax.broadcasted_iota(jnp.int32, shape, 1)
    return jnp.sum(jnp.where(same, row, 0.0), axis=1, keepdims=True)


def as_row(column):
    size = column.shape[0]
    shape = (size, size)
    same = lax.broadcasted_iota(jnp.int32, shape, 0) == lax.broadcasted_iota(jnp.int32, shape, 1)
    return jnp.sum(jnp.where(same, column, 0.0), axis=0, keepdims=True)


def merge(stats):
    highest = jnp.max(stats[:, 0:1, :], axis=0)
    total = jnp.sum(stats[:, 1:2, :] * jnp.exp(stats[:, 0:1, :] - highest[None]), axis=0)
    return highest + jnp.log(total)


def flat_half(blocks):
    count, rows, width = blocks.shape
    return blocks.astype(jnp.float32).reshape(count * rows, width).astype(jnp.bfloat16)


def kernel(
    inner_count,
    line_count,
    pair_count,
    scale_ref,
    image_hbm,
    text_hbm,
    loss_ref,
    image_grad_ref,
    text_grad_ref,
    images,
    texts,
    row_stats,
    col_stats,
    row_sums,
    col_sums,
    image_parts,
    text_parts,
    image_slots,
    text_slots,
    image_ref,
    text_ref,
    input_sems,
    line_send,
    line_recv,
    plane_send,
    plane_recv,
):
    text_in = pltpu.make_async_copy(text_hbm, text_ref, input_sems.at[0])
    image_in = pltpu.make_async_copy(image_hbm, image_ref, input_sems.at[1])
    text_in.start()
    image_in.start()
    inner, blk = lax.axis_index("inner"), lax.axis_index("blk")
    place, side = blk // pair_count, lax.rem(blk, pair_count)
    line = Group(
        place,
        line_count,
        lambda z: (inner, z * pair_count + side),
        ascending,
        (line_send, line_recv),
    )
    plane = Group(
        inner * pair_count + side,
        inner_count * pair_count,
        lambda g: (g // pair_count, place * pair_count + lax.rem(g, pair_count)),
        flipped,
        (plane_send, plane_recv),
    )
    barrier = pltpu.get_barrier_semaphore()
    meets = [group.device_of(to) for group in (plane, line) for to in group.others()]
    for to in meets:
        pl.semaphore_signal(barrier, inc=1, device_id=to, device_id_type=MESH)

    factor = scale_ref[0]
    text_in.wait()
    text_unit, text_inverse = unit_rows(text_ref[...])
    text_half = text_unit.astype(jnp.bfloat16)
    texts[plane.me] = text_half
    image_in.wait()
    image_unit, image_inverse = unit_rows(image_ref[...])
    image_half = image_unit.astype(jnp.bfloat16)
    images[line.me] = image_half
    chips = range(1, inner_count)
    near = [k for k in chips if k & (k - 1) == 0] if pair_count == 2 else list(chips)
    far = [k for k in chips if k not in near]
    chip_at = lambda k: turned(inner, inner_count, k)
    slot = lambda g, c: texts.at[g * pair_count + c]

    def text_copy(block, g, c, stage):
        return plane.copy(block, block, stage, g * pair_count + c)

    def start_texts():
        mine = slot(inner, side)
        for k in reversed(far):
            text_copy(mine, chip_at(k), side, 4).start()
        for k in near:
            for c in range(pair_count):
                text_copy(mine, chip_at(k), c, 0).start()
        if pair_count == 2:
            text_copy(mine, inner, 1 - side, 0).start()

    def some(count, stage):
        blocks = texts.at[pl.ds(0, count)]
        return plane.copy(blocks, blocks, stage, inner * pair_count + 1 - side)

    near_blocks = pair_count * len(near) + pair_count - 1

    pl.semaphore_wait(barrier, plane.size + line.size - 2)
    line.start_gather(images, 0, far_first)
    start_texts()
    image_back = image_half.astype(jnp.float32)
    text_back = text_half.astype(jnp.float32)
    diagonal = factor * jnp.sum(image_back * text_back)
    if far:
        some(len(far), 4).wait_recv()
        for k in far:
            text_copy(slot(chip_at(k), side), inner, 1 - side, 5).start()
    some(near_blocks, 0).wait_recv()
    line.wait_recv(images, 0)
    if far:
        some(len(far), 5).wait_recv()

    image_group = flat_half(images[...])
    text_group = flat_half(texts[...])
    image_count, text_count = image_group.shape[0], text_group.shape[0]
    turned_logits = factor * lax.dot_general(
        text_group, image_group, (((1,), (1,)), ((), ())), preferred_element_type=jnp.float32
    )
    row_peak = jnp.max(turned_logits, axis=0, keepdims=True)
    row_total = jnp.sum(jnp.exp(turned_logits - row_peak), axis=0, keepdims=True)
    row_stats[line.me, 0:1, :] = row_peak
    row_stats[line.me, 1:2, :] = row_total
    line.start_gather(row_stats, 1, far_first)
    logits = factor * lax.dot_general(
        image_group, text_group, (((1,), (1,)), ((), ())), preferred_element_type=jnp.float32
    )
    col_peak = jnp.max(logits, axis=0, keepdims=True)
    col_total = jnp.sum(jnp.exp(logits - col_peak), axis=0, keepdims=True)
    col_stats[plane.me, 0:1, :] = col_peak
    col_stats[plane.me, 1:2, :] = col_total
    col_stats[plane.me, 2:3, :] = jnp.full((1, text_count), diagonal, jnp.float32)
    plane.start_gather(col_stats, 1)
    plane.wait_recv(col_stats, 1)
    col_lse = merge(col_stats[...])
    col_weights = jnp.exp(logits - col_lse)
    turned_weights = jnp.exp(turned_logits - as_column(col_lse))
    line.wait_recv(row_stats, 1)
    row_lse = merge(row_stats[...])

    weights = (
        0.5 * factor * (jnp.exp(logits - as_column(row_lse)) + col_weights)
    ).astype(jnp.bfloat16)
    image_parts[...] = (
        jnp.dot(weights, text_group, preferred_element_type=jnp.float32)
        .reshape(image_parts.shape)
        .astype(jnp.bfloat16)
    )
    line.start_scatter(image_parts, image_slots, 2, part=slice(0, 1))
    turned_weights = (
        0.5 * factor * (jnp.exp(turned_logits - row_lse) + turned_weights)
    ).astype(jnp.bfloat16)
    text_parts[...] = (
        jnp.dot(turned_weights, image_group, preferred_element_type=jnp.float32)
        .reshape(text_parts.shape)
        .astype(jnp.bfloat16)
    )
    plane.start_scatter(text_parts, text_slots, 2, ascending, slice(0, pair_count))
    tile = row_sums.shape[1:]
    plane_diagonal = jnp.sum(col_stats[:, 2, 0:1])
    row_sums[plane.me] = jnp.full(tile, jnp.sum(row_lse), jnp.float32)
    col_sums[line.me] = jnp.full(tile, jnp.sum(col_lse) - 2.0 * plane_diagonal, jnp.float32)
    plane.start_gather(row_sums, 3)
    line.start_gather(col_sums, 3)
    line.wait_some(image_parts, 2, 1)
    line.start_scatter(image_parts, image_slots, 2, part=slice(1, None), later=4)
    plane.start_scatter(text_parts, text_slots, 2, ascending, slice(pair_count, None), 6)

    rows = image_ref.shape[0]
    plane.wait_recv(text_slots, 2)
    text_sum = text_parts[plane.me].astype(jnp.float32)
    for other in plane.others():
        text_sum = text_sum + text_slots[other].astype(jnp.float32)
    text_grad_ref[...] = project(text_sum - factor * image_back, text_unit, text_inverse)
    line.wait_recv(image_slots, 2)
    image_sum = image_parts[line.me].astype(jnp.float32)
    for other in line.others():
        image_sum = image_sum + image_slots[other].astype(jnp.float32)
    image_grad_ref[...] = project(image_sum - factor * text_back, image_unit, image_inverse)

    plane.wait_recv(row_sums, 3)
    line.wait_recv(col_sums, 3)
    examples = 2.0 * line.size * plane.size * rows
    whole = jnp.sum(row_sums[...], axis=0)[0:1, 0:1] + jnp.sum(col_sums[...], axis=0)[0:1, 0:1]
    loss_ref[...] = jnp.broadcast_to(whole / examples, loss_ref.shape)
    plane.wait_some(text_parts, 2, pair_count)
    line.wait_some(image_parts, 4, line_count - 2)
    plane.wait_some(text_parts, 6, plane.size - 1 - pair_count)
    line.wait_send(images, 0)
    some(near_blocks, 0).wait_send()
    if far:
        some(len(far), 4).wait_send()
        some(len(far), 5).wait_send()
    for buf_line, buf_plane, stage in (
        (row_stats, col_stats, 1),
        (col_sums, row_sums, 3),
    ):
        line.wait_send(buf_line, stage)
        plane.wait_send(buf_plane, stage)


def store(loss, image_grad, text_grad, loss_hbm, image_hbm, text_hbm, sems):
    pairs = ((image_grad, image_hbm), (text_grad, text_hbm), (loss, loss_hbm))
    copies = [pltpu.make_async_copy(*pair, sems.at[k]) for k, pair in enumerate(pairs)]
    for copy in copies:
        copy.start()
    for copy in copies:
        copy.wait()


def solution(mesh):
    inner_count, blk_count = mesh.shape["inner"], mesh.shape["blk"]
    pair_count = 2 if blk_count % 2 == 0 else 1
    line_count = blk_count // pair_count
    plane_count = inner_count * pair_count

    def on_device(image_emb, text_emb, logit_scale):
        rows, width = image_emb.shape
        vmem = pl.BlockSpec(memory_space=pltpu.VMEM)
        hbm = pl.BlockSpec(memory_space=pl.ANY)
        smem = pl.BlockSpec(memory_space=pltpu.SMEM)
        near = pltpu.VMEM((rows, width), jnp.float32)
        results = pl.pallas_call(
            functools.partial(kernel, inner_count, line_count, pair_count),
            out_shape=(pltpu.VMEM((1, 128), jnp.float32), near, near),
            in_specs=[smem, hbm, hbm],
            out_specs=(vmem, vmem, vmem),
            scratch_shapes=[
                pltpu.VMEM((line_count, rows, width), jnp.bfloat16),
                pltpu.VMEM((plane_count, rows, width), jnp.bfloat16),
                pltpu.VMEM((line_count, 2, line_count * rows), jnp.float32),
                pltpu.VMEM((plane_count, 4, plane_count * rows), jnp.float32),
                pltpu.VMEM((plane_count, 1, 128), jnp.float32),
                pltpu.VMEM((line_count, 1, 128), jnp.float32),
                pltpu.VMEM((line_count, rows, width), jnp.bfloat16),
                pltpu.VMEM((plane_count, rows, width), jnp.bfloat16),
                pltpu.VMEM((line_count, rows, width), jnp.bfloat16),
                pltpu.VMEM((plane_count, rows, width), jnp.bfloat16),
                pltpu.VMEM((rows, width), jnp.float32),
                pltpu.VMEM((rows, width), jnp.float32),
                pltpu.SemaphoreType.DMA((2,)),
                pltpu.SemaphoreType.DMA((5,)),
                pltpu.SemaphoreType.DMA((5,)),
                pltpu.SemaphoreType.DMA((7,)),
                pltpu.SemaphoreType.DMA((7,)),
            ],
            compiler_params=pltpu.CompilerParams(
                collective_id=0, has_side_effects=True, vmem_limit_bytes=56 * 1024 * 1024
            ),
            name="contrastive",
        )(logit_scale, image_emb, text_emb)
        far = jax.ShapeDtypeStruct((rows, width), jnp.float32)
        loss, image_grad, text_grad = pl.pallas_call(
            store,
            out_shape=(jax.ShapeDtypeStruct((1, 128), jnp.float32), far, far),
            in_specs=[vmem, vmem, vmem],
            out_specs=(hbm, hbm, hbm),
            scratch_shapes=[pltpu.SemaphoreType.DMA((3,))],
            compiler_params=pltpu.CompilerParams(vmem_limit_bytes=16 * 1024 * 1024),
            name="store",
        )(*results)
        return loss.reshape(128)[0:1], image_grad, text_grad

    in_specs = (P(("inner", "blk"), None), P(("inner", "blk"), None), P())
    out_specs = (P(), P(("inner", "blk"), None), P(("inner", "blk"), None))
    return jax.shard_map(
        on_device, mesh=mesh, in_specs=in_specs, out_specs=out_specs, check_vma=False
    )
```

```python
import functools

import jax
import jax.numpy as jnp
from jax import lax
from jax.experimental import pallas as pl
from jax.experimental.pallas import tpu as pltpu
from jax.sharding import PartitionSpec as P

EPSILON = 1e-06
MESH = pl.DeviceIdType.MESH


def unit_rows(values):
    inverse = lax.rsqrt(jnp.sum(values * values, axis=1, keepdims=True) + EPSILON)
    return (values * inverse, inverse)


def project(gradient, direction, inverse):
    return (gradient - direction * jnp.sum(gradient * direction, axis=1, keepdims=True)) * inverse


class Group:
    def __init__(self, me, size, device_of, order, sems):
        self.me, self.size, self.device_of, self.sems = me, size, device_of, sems
        self.order = order

    def others(self, order=None):
        order = order or self.order
        return [order(self.me, self.size, k) for k in range(1, self.size)]

    def copy(self, src, dst, stage, to, later=None):
        send_sems, recv_sems = self.sems
        return pltpu.make_async_remote_copy(
            src_ref=src,
            dst_ref=dst,
            send_sem=send_sems.at[stage if later is None else later],
            recv_sem=recv_sems.at[stage],
            device_id=self.device_of(to),
            device_id_type=MESH,
        )

    def whole(self, buf, stage):
        part = buf.at[pl.ds(0, self.size - 1)]
        return self.copy(part, part, stage, self.order(self.me, self.size, 1))

    def start_gather(self, buf, stage, order=None):
        mine = buf.at[self.me]
        for to in self.others(order):
            self.copy(mine, mine, stage, to).start()

    def wait_recv(self, buf, stage):
        self.whole(buf, stage).wait_recv()

    def wait_send(self, buf, stage):
        self.whole(buf, stage).wait_send()

    def wait_some(self, buf, stage, count):
        part = buf.at[pl.ds(0, count)]
        self.copy(part, part, stage, self.order(self.me, self.size, 1)).wait_send()

    def start_scatter(self, parts, slots, stage, order=None, part=slice(None), later=None):
        for to in self.others(order)[part]:
            self.copy(parts.at[to], slots.at[self.me], stage, to, later).start()


def ascending(me, size, k):
    return k - 1 + (k - 1 >= me).astype(jnp.int32)


def far_first(me, size, k):
    low = size - k - (size - k <= me).astype(jnp.int32)
    return jnp.where(2 * me < size, low, ascending(me, size, k))


def turned(me, size, k):
    if size & (size - 1):
        return lax.rem(me + k, size)
    out, bit = me, 1
    while bit <= k:
        if k & bit:
            out = out + bit * (1 - 2 * lax.rem(me // bit, 2))
        bit *= 2
    return out


def flipped(me, size, k):
    return turned(me, size, size - k)


def as_column(row):
    size = row.shape[1]
    shape = (size, size)
    same = lax.broadcasted_iota(jnp.int32, shape, 0) == lax.broadcasted_iota(jnp.int32, shape, 1)
    return jnp.sum(jnp.where(same, row, 0.0), axis=1, keepdims=True)


def as_row(column):
    size = column.shape[0]
    shape = (size, size)
    same = lax.broadcasted_iota(jnp.int32, shape, 0) == lax.broadcasted_iota(jnp.int32, shape, 1)
    return jnp.sum(jnp.where(same, column, 0.0), axis=0, keepdims=True)


def merge(stats):
    highest = jnp.max(stats[:, 0:1, :], axis=0)
    total = jnp.sum(stats[:, 1:2, :] * jnp.exp(stats[:, 0:1, :] - highest[None]), axis=0)
    return highest + jnp.log(total)


def flat_half(blocks):
    count, rows, width = blocks.shape
    return blocks.astype(jnp.float32).reshape(count * rows, width).astype(jnp.bfloat16)


def kernel(
    inner_count,
    line_count,
    pair_count,
    scale_ref,
    image_hbm,
    text_hbm,
    loss_ref,
    image_grad_ref,
    text_grad_ref,
    images,
    texts,
    row_stats,
    col_stats,
    row_sums,
    col_sums,
    image_parts,
    text_parts,
    image_slots,
    text_slots,
    image_ref,
    text_ref,
    input_sems,
    line_send,
    line_recv,
    plane_send,
    plane_recv,
):
    text_in = pltpu.make_async_copy(text_hbm, text_ref, input_sems.at[0])
    image_in = pltpu.make_async_copy(image_hbm, image_ref, input_sems.at[1])
    text_in.start()
    image_in.start()
    inner, blk = lax.axis_index("inner"), lax.axis_index("blk")
    place, side = blk // pair_count, lax.rem(blk, pair_count)
    line = Group(
        place,
        line_count,
        lambda z: (inner, z * pair_count + side),
        ascending,
        (line_send, line_recv),
    )
    plane = Group(
        inner * pair_count + side,
        inner_count * pair_count,
        lambda g: (g // pair_count, place * pair_count + lax.rem(g, pair_count)),
        flipped,
        (plane_send, plane_recv),
    )
    barrier = pltpu.get_barrier_semaphore()
    meets = [group.device_of(to) for group in (plane, line) for to in group.others()]
    for to in meets:
        pl.semaphore_signal(barrier, inc=1, device_id=to, device_id_type=MESH)

    factor = scale_ref[0]
    text_in.wait()
    text_unit, text_inverse = unit_rows(text_ref[...])
    text_half = text_unit.astype(jnp.bfloat16)
    texts[plane.me] = text_half
    image_in.wait()
    image_unit, image_inverse = unit_rows(image_ref[...])
    image_half = image_unit.astype(jnp.bfloat16)
    images[line.me] = image_half
    chips = range(1, inner_count)
    near = [k for k in chips if k & (k - 1) == 0] if pair_count == 2 else list(chips)
    far = [k for k in chips if k not in near]
    chip_at = lambda k: turned(inner, inner_count, k)
    slot = lambda g, c: texts.at[g * pair_count + c]

    def text_copy(block, g, c, stage):
        return plane.copy(block, block, stage, g * pair_count + c, 0)

    def start_texts():
        mine = slot(inner, side)
        for k in reversed(far):
            text_copy(mine, chip_at(k), side, 4).start()
        for k in near:
            for c in range(pair_count):
                text_copy(mine, chip_at(k), c, 0).start()
        if pair_count == 2:
            text_copy(mine, inner, 1 - side, 0).start()

    def some(count, stage):
        blocks = texts.at[pl.ds(0, count)]
        return plane.copy(blocks, blocks, stage, inner * pair_count + 1 - side)

    near_blocks = pair_count * len(near) + pair_count - 1

    pl.semaphore_wait(barrier, plane.size + line.size - 2)
    line.start_gather(images, 0, far_first)
    start_texts()
    image_back = image_half.astype(jnp.float32)
    text_back = text_half.astype(jnp.float32)
    diagonal = factor * jnp.sum(image_back * text_back)
    if far:
        some(len(far), 4).wait_recv()
        for k in far:
            text_copy(slot(chip_at(k), side), inner, 1 - side, 5).start()
    some(near_blocks, 0).wait_recv()
    if far:
        some(len(far), 5).wait_recv()
    text_group = flat_half(texts[...])
    line.wait_recv(images, 0)

    image_group = flat_half(images[...])
    image_count, text_count = image_group.shape[0], text_group.shape[0]
    turned_logits = factor * lax.dot_general(
        text_group, image_group, (((1,), (1,)), ((), ())), preferred_element_type=jnp.float32
    )
    row_peak = jnp.max(turned_logits, axis=0, keepdims=True)
    row_total = jnp.sum(jnp.exp(turned_logits - row_peak), axis=0, keepdims=True)
    row_stats[line.me, 0:1, :] = row_peak
    row_stats[line.me, 1:2, :] = row_total
    line.start_gather(row_stats, 1, far_first)
    logits = factor * lax.dot_general(
        image_group, text_group, (((1,), (1,)), ((), ())), preferred_element_type=jnp.float32
    )
    col_peak = jnp.max(logits, axis=0, keepdims=True)
    col_total = jnp.sum(jnp.exp(logits - col_peak), axis=0, keepdims=True)
    col_stats[plane.me, 0:1, :] = col_peak
    col_stats[plane.me, 1:2, :] = col_total
    col_stats[plane.me, 2:3, :] = jnp.full((1, text_count), diagonal, jnp.float32)
    plane.start_gather(col_stats, 1)
    plane.wait_recv(col_stats, 1)
    col_lse = merge(col_stats[...])
    col_weights = jnp.exp(logits - col_lse)
    turned_weights = jnp.exp(turned_logits - as_column(col_lse))
    line.wait_recv(row_stats, 1)
    row_lse = merge(row_stats[...])

    weights = (
        0.5 * factor * (jnp.exp(logits - as_column(row_lse)) + col_weights)
    ).astype(jnp.bfloat16)
    image_parts[...] = (
        jnp.dot(weights, text_group, preferred_element_type=jnp.float32)
        .reshape(image_parts.shape)
        .astype(jnp.bfloat16)
    )
    line.start_scatter(image_parts, image_slots, 2, part=slice(0, 1))
    turned_weights = (
        0.5 * factor * (jnp.exp(turned_logits - row_lse) + turned_weights)
    ).astype(jnp.bfloat16)
    text_parts[...] = (
        jnp.dot(turned_weights, image_group, preferred_element_type=jnp.float32)
        .reshape(text_parts.shape)
        .astype(jnp.bfloat16)
    )
    plane.start_scatter(text_parts, text_slots, 2, ascending, slice(0, pair_count))
    tile = row_sums.shape[1:]
    plane_diagonal = jnp.sum(col_stats[:, 2, 0:1])
    row_sums[plane.me] = jnp.full(tile, jnp.sum(row_lse), jnp.float32)
    col_sums[line.me] = jnp.full(tile, jnp.sum(col_lse) - 2.0 * plane_diagonal, jnp.float32)
    plane.start_gather(row_sums, 3)
    line.start_gather(col_sums, 3)
    line.wait_some(image_parts, 2, 1)
    line.start_scatter(image_parts, image_slots, 2, part=slice(1, None), later=4)
    plane.start_scatter(text_parts, text_slots, 2, ascending, slice(pair_count, None), 4)

    rows = image_ref.shape[0]
    plane.wait_recv(text_slots, 2)
    text_sum = text_parts[plane.me].astype(jnp.float32)
    for other in plane.others():
        text_sum = text_sum + text_slots[other].astype(jnp.float32)
    text_grad_ref[...] = project(text_sum - factor * image_back, text_unit, text_inverse)
    line.wait_recv(image_slots, 2)
    image_sum = image_parts[line.me].astype(jnp.float32)
    for other in line.others():
        image_sum = image_sum + image_slots[other].astype(jnp.float32)
    image_grad_ref[...] = project(image_sum - factor * text_back, image_unit, image_inverse)

    plane.wait_recv(row_sums, 3)
    line.wait_recv(col_sums, 3)
    examples = 2.0 * line.size * plane.size * rows
    whole = jnp.sum(row_sums[...], axis=0)[0:1, 0:1] + jnp.sum(col_sums[...], axis=0)[0:1, 0:1]
    loss_ref[...] = jnp.broadcast_to(whole / examples, loss_ref.shape)
    plane.wait_some(text_parts, 2, pair_count)
    line.wait_some(image_parts, 4, line_count - 2)
    plane.wait_some(text_parts, 4, plane.size - 1 - pair_count)
    line.wait_send(images, 0)
    some(near_blocks + 2 * len(far), 0).wait_send()
    for buf_line, buf_plane, stage in (
        (row_stats, col_stats, 1),
        (col_sums, row_sums, 3),
    ):
        line.wait_send(buf_line, stage)
        plane.wait_send(buf_plane, stage)


def store(loss, image_grad, text_grad, loss_hbm, image_hbm, text_hbm, sems):
    pairs = ((image_grad, image_hbm), (text_grad, text_hbm), (loss, loss_hbm))
    copies = [pltpu.make_async_copy(*pair, sems.at[k]) for k, pair in enumerate(pairs)]
    for copy in copies:
        copy.start()
    for copy in copies:
        copy.wait()


def solution(mesh):
    inner_count, blk_count = mesh.shape["inner"], mesh.shape["blk"]
    pair_count = 2 if blk_count % 2 == 0 else 1
    line_count = blk_count // pair_count
    plane_count = inner_count * pair_count

    def on_device(image_emb, text_emb, logit_scale):
        rows, width = image_emb.shape
        vmem = pl.BlockSpec(memory_space=pltpu.VMEM)
        hbm = pl.BlockSpec(memory_space=pl.ANY)
        smem = pl.BlockSpec(memory_space=pltpu.SMEM)
        near = pltpu.VMEM((rows, width), jnp.float32)
        results = pl.pallas_call(
            functools.partial(kernel, inner_count, line_count, pair_count),
            out_shape=(pltpu.VMEM((1, 128), jnp.float32), near, near),
            in_specs=[smem, hbm, hbm],
            out_specs=(vmem, vmem, vmem),
            scratch_shapes=[
                pltpu.VMEM((line_count, rows, width), jnp.bfloat16),
                pltpu.VMEM((plane_count, rows, width), jnp.bfloat16),
                pltpu.VMEM((line_count, 2, line_count * rows), jnp.float32),
                pltpu.VMEM((plane_count, 4, plane_count * rows), jnp.float32),
                pltpu.VMEM((plane_count, 1, 128), jnp.float32),
                pltpu.VMEM((line_count, 1, 128), jnp.float32),
                pltpu.VMEM((line_count, rows, width), jnp.bfloat16),
                pltpu.VMEM((plane_count, rows, width), jnp.bfloat16),
                pltpu.VMEM((line_count, rows, width), jnp.bfloat16),
                pltpu.VMEM((plane_count, rows, width), jnp.bfloat16),
                pltpu.VMEM((rows, width), jnp.float32),
                pltpu.VMEM((rows, width), jnp.float32),
                pltpu.SemaphoreType.DMA((2,)),
                pltpu.SemaphoreType.DMA((5,)),
                pltpu.SemaphoreType.DMA((4,)),
                pltpu.SemaphoreType.DMA((5,)),
                pltpu.SemaphoreType.DMA((6,)),
            ],
            compiler_params=pltpu.CompilerParams(
                collective_id=0, has_side_effects=True, vmem_limit_bytes=56 * 1024 * 1024
            ),
            name="contrastive",
        )(logit_scale, image_emb, text_emb)
        far = jax.ShapeDtypeStruct((rows, width), jnp.float32)
        loss, image_grad, text_grad = pl.pallas_call(
            store,
            out_shape=(jax.ShapeDtypeStruct((1, 128), jnp.float32), far, far),
            in_specs=[vmem, vmem, vmem],
            out_specs=(hbm, hbm, hbm),
            scratch_shapes=[pltpu.SemaphoreType.DMA((3,))],
            compiler_params=pltpu.CompilerParams(vmem_limit_bytes=16 * 1024 * 1024),
            name="store",
        )(*results)
        return loss.reshape(128)[0:1], image_grad, text_grad

    in_specs = (P(("inner", "blk"), None), P(("inner", "blk"), None), P())
    out_specs = (P(), P(("inner", "blk"), None), P(("inner", "blk"), None))
    return jax.shard_map(
        on_device, mesh=mesh, in_specs=in_specs, out_specs=out_specs, check_vma=False
    )
```

```python
import functools

import jax
import jax.numpy as jnp
from jax import lax
from jax.experimental import pallas as pl
from jax.experimental.pallas import tpu as pltpu
from jax.sharding import PartitionSpec as P

EPSILON = 1e-06
MESH = pl.DeviceIdType.MESH


def unit_rows(values):
    inverse = lax.rsqrt(jnp.sum(values * values, axis=1, keepdims=True) + EPSILON)
    return (values * inverse, inverse)


def project(gradient, direction, inverse):
    return (gradient - direction * jnp.sum(gradient * direction, axis=1, keepdims=True)) * inverse


class Group:
    def __init__(self, me, size, device_of, order, sems):
        self.me, self.size, self.device_of, self.sems = me, size, device_of, sems
        self.order = order

    def others(self, order=None):
        order = order or self.order
        return [order(self.me, self.size, k) for k in range(1, self.size)]

    def copy(self, src, dst, stage, to, later=None):
        send_sems, recv_sems = self.sems
        return pltpu.make_async_remote_copy(
            src_ref=src,
            dst_ref=dst,
            send_sem=send_sems.at[stage if later is None else later],
            recv_sem=recv_sems.at[stage],
            device_id=self.device_of(to),
            device_id_type=MESH,
        )

    def whole(self, buf, stage):
        part = buf.at[pl.ds(0, self.size - 1)]
        return self.copy(part, part, stage, self.order(self.me, self.size, 1))

    def start_gather(self, buf, stage, order=None):
        mine = buf.at[self.me]
        for to in self.others(order):
            self.copy(mine, mine, stage, to).start()

    def wait_recv(self, buf, stage):
        self.whole(buf, stage).wait_recv()

    def wait_send(self, buf, stage):
        self.whole(buf, stage).wait_send()

    def wait_some(self, buf, stage, count):
        part = buf.at[pl.ds(0, count)]
        self.copy(part, part, stage, self.order(self.me, self.size, 1)).wait_send()

    def start_scatter(self, parts, slots, stage, order=None, part=slice(None), later=None):
        for to in self.others(order)[part]:
            self.copy(parts.at[to], slots.at[self.me], stage, to, later).start()


def ascending(me, size, k):
    return k - 1 + (k - 1 >= me).astype(jnp.int32)


def far_first(me, size, k):
    low = size - k - (size - k <= me).astype(jnp.int32)
    return jnp.where(2 * me < size, low, ascending(me, size, k))


def turned(me, size, k):
    if size & (size - 1):
        return lax.rem(me + k, size)
    out, bit = me, 1
    while bit <= k:
        if k & bit:
            out = out + bit * (1 - 2 * lax.rem(me // bit, 2))
        bit *= 2
    return out


def flipped(me, size, k):
    return turned(me, size, size - k)


def as_column(row):
    size = row.shape[1]
    shape = (size, size)
    same = lax.broadcasted_iota(jnp.int32, shape, 0) == lax.broadcasted_iota(jnp.int32, shape, 1)
    return jnp.sum(jnp.where(same, row, 0.0), axis=1, keepdims=True)


def as_row(column):
    size = column.shape[0]
    shape = (size, size)
    same = lax.broadcasted_iota(jnp.int32, shape, 0) == lax.broadcasted_iota(jnp.int32, shape, 1)
    return jnp.sum(jnp.where(same, column, 0.0), axis=0, keepdims=True)


def merge(stats):
    highest = jnp.max(stats[:, 0:1, :], axis=0)
    total = jnp.sum(stats[:, 1:2, :] * jnp.exp(stats[:, 0:1, :] - highest[None]), axis=0)
    return highest + jnp.log(total)


def flat_half(blocks):
    count, rows, width = blocks.shape
    return blocks.astype(jnp.float32).reshape(count * rows, width).astype(jnp.bfloat16)


def kernel(
    inner_count,
    line_count,
    pair_count,
    scale_ref,
    image_hbm,
    text_hbm,
    loss_ref,
    image_grad_ref,
    text_grad_ref,
    images,
    texts,
    row_stats,
    col_stats,
    row_sums,
    col_sums,
    image_parts,
    text_parts,
    image_slots,
    text_slots,
    image_ref,
    text_ref,
    input_sems,
    line_send,
    line_recv,
    plane_send,
    plane_recv,
):
    text_in = pltpu.make_async_copy(text_hbm, text_ref, input_sems.at[0])
    image_in = pltpu.make_async_copy(image_hbm, image_ref, input_sems.at[1])
    text_in.start()
    image_in.start()
    inner, blk = lax.axis_index("inner"), lax.axis_index("blk")
    place, side = blk // pair_count, lax.rem(blk, pair_count)
    line = Group(
        place,
        line_count,
        lambda z: (inner, z * pair_count + side),
        ascending,
        (line_send, line_recv),
    )
    plane = Group(
        inner * pair_count + side,
        inner_count * pair_count,
        lambda g: (g // pair_count, place * pair_count + lax.rem(g, pair_count)),
        flipped,
        (plane_send, plane_recv),
    )
    barrier = pltpu.get_barrier_semaphore()
    meets = [group.device_of(to) for group in (plane, line) for to in group.others()]
    for to in meets:
        pl.semaphore_signal(barrier, inc=1, device_id=to, device_id_type=MESH)

    factor = scale_ref[0]
    text_in.wait()
    text_unit, text_inverse = unit_rows(text_ref[...])
    text_half = text_unit.astype(jnp.bfloat16)
    texts[plane.me] = text_half
    image_in.wait()
    image_unit, image_inverse = unit_rows(image_ref[...])
    image_half = image_unit.astype(jnp.bfloat16)
    images[line.me] = image_half
    chips = range(1, inner_count)
    near = [k for k in chips if k & (k - 1) == 0] if pair_count == 2 else list(chips)
    far = [k for k in chips if k not in near]
    chip_at = lambda k: turned(inner, inner_count, k)
    slot = lambda g, c: texts.at[g * pair_count + c]

    def text_copy(block, g, c, stage):
        return plane.copy(block, block, stage, g * pair_count + c, 0)

    def start_texts():
        mine = slot(inner, side)
        for k in reversed(far):
            text_copy(mine, chip_at(k), side, 4).start()
        for k in near:
            for c in range(pair_count):
                text_copy(mine, chip_at(k), c, 0).start()
        if pair_count == 2:
            text_copy(mine, inner, 1 - side, 0).start()

    def some(count, stage):
        blocks = texts.at[pl.ds(0, count)]
        return plane.copy(blocks, blocks, stage, inner * pair_count + 1 - side)

    near_blocks = pair_count * len(near) + pair_count - 1

    pl.semaphore_wait(barrier, plane.size + line.size - 2)
    line.start_gather(images, 0, far_first)
    start_texts()
    image_back = image_half.astype(jnp.float32)
    text_back = text_half.astype(jnp.float32)
    diagonal = factor * jnp.sum(image_back * text_back)
    if far:
        some(len(far), 4).wait_recv()
        for k in far:
            text_copy(slot(chip_at(k), side), inner, 1 - side, 5).start()
    some(near_blocks, 0).wait_recv()
    if far:
        some(len(far), 5).wait_recv()
    text_group = flat_half(texts[...])
    line.wait_recv(images, 0)

    image_group = flat_half(images[...])
    image_count, text_count = image_group.shape[0], text_group.shape[0]
    turned_logits = factor * lax.dot_general(
        text_group, image_group, (((1,), (1,)), ((), ())), preferred_element_type=jnp.float32
    )
    row_peak = jnp.max(turned_logits, axis=0, keepdims=True)
    row_total = jnp.sum(jnp.exp(turned_logits - row_peak), axis=0, keepdims=True)
    row_stats[line.me, 0:1, :] = row_peak
    row_stats[line.me, 1:2, :] = row_total
    line.start_gather(row_stats, 1, far_first)
    logits = factor * lax.dot_general(
        image_group, text_group, (((1,), (1,)), ((), ())), preferred_element_type=jnp.float32
    )
    col_peak = jnp.max(logits, axis=0, keepdims=True)
    col_total = jnp.sum(jnp.exp(logits - col_peak), axis=0, keepdims=True)
    col_stats[plane.me, 0:1, :] = col_peak
    col_stats[plane.me, 1:2, :] = col_total
    col_stats[plane.me, 2:3, :] = jnp.full((1, text_count), diagonal, jnp.float32)
    plane.start_gather(col_stats, 1)
    plane.wait_recv(col_stats, 1)
    col_lse = merge(col_stats[...])
    col_weights = jnp.exp(logits - col_lse)
    turned_weights = jnp.exp(turned_logits - as_column(col_lse))
    line.wait_recv(row_stats, 1)
    row_lse = merge(row_stats[...])

    weights = (
        0.5 * factor * (jnp.exp(logits - as_column(row_lse)) + col_weights)
    ).astype(jnp.bfloat16)
    image_parts[...] = (
        jnp.dot(weights, text_group, preferred_element_type=jnp.float32)
        .reshape(image_parts.shape)
        .astype(jnp.bfloat16)
    )
    line.start_scatter(image_parts, image_slots, 2, part=slice(0, 1))
    turned_weights = (
        0.5 * factor * (jnp.exp(turned_logits - row_lse) + turned_weights)
    ).astype(jnp.bfloat16)
    text_parts[...] = (
        jnp.dot(turned_weights, image_group, preferred_element_type=jnp.float32)
        .reshape(text_parts.shape)
        .astype(jnp.bfloat16)
    )
    plane.start_scatter(text_parts, text_slots, 2, ascending, slice(0, pair_count))
    tile = row_sums.shape[1:]
    plane_diagonal = jnp.sum(col_stats[:, 2, 0:1])
    row_sums[plane.me] = jnp.full(tile, jnp.sum(row_lse), jnp.float32)
    col_sums[line.me] = jnp.full(tile, jnp.sum(col_lse) - 2.0 * plane_diagonal, jnp.float32)
    plane.start_gather(row_sums, 3)
    line.start_gather(col_sums, 3)

    held = place == line_count - 1

    @pl.when(held)
    def _():
        line.wait_some(image_parts, 2, 1)

    line.start_scatter(image_parts, image_slots, 2, part=slice(1, None), later=4)
    plane.start_scatter(text_parts, text_slots, 2, ascending, slice(pair_count, None), 4)

    rows = image_ref.shape[0]
    plane.wait_recv(text_slots, 2)
    text_sum = text_parts[plane.me].astype(jnp.float32)
    for other in plane.others():
        text_sum = text_sum + text_slots[other].astype(jnp.float32)
    text_grad_ref[...] = project(text_sum - factor * image_back, text_unit, text_inverse)
    line.wait_recv(image_slots, 2)
    image_sum = image_parts[line.me].astype(jnp.float32)
    for other in line.others():
        image_sum = image_sum + image_slots[other].astype(jnp.float32)
    image_grad_ref[...] = project(image_sum - factor * text_back, image_unit, image_inverse)

    plane.wait_recv(row_sums, 3)
    line.wait_recv(col_sums, 3)
    examples = 2.0 * line.size * plane.size * rows
    whole = jnp.sum(row_sums[...], axis=0)[0:1, 0:1] + jnp.sum(col_sums[...], axis=0)[0:1, 0:1]
    loss_ref[...] = jnp.broadcast_to(whole / examples, loss_ref.shape)
    plane.wait_some(text_parts, 2, pair_count)

    @pl.when(jnp.logical_not(held))
    def _():
        line.wait_some(image_parts, 2, 1)

    line.wait_some(image_parts, 4, line_count - 2)
    plane.wait_some(text_parts, 4, plane.size - 1 - pair_count)
    line.wait_send(images, 0)
    some(near_blocks + 2 * len(far), 0).wait_send()
    for buf_line, buf_plane, stage in (
        (row_stats, col_stats, 1),
        (col_sums, row_sums, 3),
    ):
        line.wait_send(buf_line, stage)
        plane.wait_send(buf_plane, stage)


def store(loss, image_grad, text_grad, loss_hbm, image_hbm, text_hbm, sems):
    pairs = ((image_grad, image_hbm), (text_grad, text_hbm), (loss, loss_hbm))
    copies = [pltpu.make_async_copy(*pair, sems.at[k]) for k, pair in enumerate(pairs)]
    for copy in copies:
        copy.start()
    for copy in copies:
        copy.wait()


def solution(mesh):
    inner_count, blk_count = mesh.shape["inner"], mesh.shape["blk"]
    pair_count = 2 if blk_count % 2 == 0 else 1
    line_count = blk_count // pair_count
    plane_count = inner_count * pair_count

    def on_device(image_emb, text_emb, logit_scale):
        rows, width = image_emb.shape
        vmem = pl.BlockSpec(memory_space=pltpu.VMEM)
        hbm = pl.BlockSpec(memory_space=pl.ANY)
        smem = pl.BlockSpec(memory_space=pltpu.SMEM)
        near = pltpu.VMEM((rows, width), jnp.float32)
        results = pl.pallas_call(
            functools.partial(kernel, inner_count, line_count, pair_count),
            out_shape=(pltpu.VMEM((1, 128), jnp.float32), near, near),
            in_specs=[smem, hbm, hbm],
            out_specs=(vmem, vmem, vmem),
            scratch_shapes=[
                pltpu.VMEM((line_count, rows, width), jnp.bfloat16),
                pltpu.VMEM((plane_count, rows, width), jnp.bfloat16),
                pltpu.VMEM((line_count, 2, line_count * rows), jnp.float32),
                pltpu.VMEM((plane_count, 4, plane_count * rows), jnp.float32),
                pltpu.VMEM((plane_count, 1, 128), jnp.float32),
                pltpu.VMEM((line_count, 1, 128), jnp.float32),
                pltpu.VMEM((line_count, rows, width), jnp.bfloat16),
                pltpu.VMEM((plane_count, rows, width), jnp.bfloat16),
                pltpu.VMEM((line_count, rows, width), jnp.bfloat16),
                pltpu.VMEM((plane_count, rows, width), jnp.bfloat16),
                pltpu.VMEM((rows, width), jnp.float32),
                pltpu.VMEM((rows, width), jnp.float32),
                pltpu.SemaphoreType.DMA((2,)),
                pltpu.SemaphoreType.DMA((5,)),
                pltpu.SemaphoreType.DMA((4,)),
                pltpu.SemaphoreType.DMA((5,)),
                pltpu.SemaphoreType.DMA((6,)),
            ],
            compiler_params=pltpu.CompilerParams(
                collective_id=0, has_side_effects=True, vmem_limit_bytes=56 * 1024 * 1024
            ),
            name="contrastive",
        )(logit_scale, image_emb, text_emb)
        far = jax.ShapeDtypeStruct((rows, width), jnp.float32)
        loss, image_grad, text_grad = pl.pallas_call(
            store,
            out_shape=(jax.ShapeDtypeStruct((1, 128), jnp.float32), far, far),
            in_specs=[vmem, vmem, vmem],
            out_specs=(hbm, hbm, hbm),
            scratch_shapes=[pltpu.SemaphoreType.DMA((3,))],
            compiler_params=pltpu.CompilerParams(vmem_limit_bytes=16 * 1024 * 1024),
            name="store",
        )(*results)
        return loss.reshape(128)[0:1], image_grad, text_grad

    in_specs = (P(("inner", "blk"), None), P(("inner", "blk"), None), P())
    out_specs = (P(), P(("inner", "blk"), None), P(("inner", "blk"), None))
    return jax.shard_map(
        on_device, mesh=mesh, in_specs=in_specs, out_specs=out_specs, check_vma=False
    )
```

```python
import functools

import jax
import jax.numpy as jnp
from jax import lax
from jax.experimental import pallas as pl
from jax.experimental.pallas import tpu as pltpu
from jax.sharding import PartitionSpec as P

EPSILON = 1e-06
MESH = pl.DeviceIdType.MESH


def unit_rows(values):
    inverse = lax.rsqrt(jnp.sum(values * values, axis=1, keepdims=True) + EPSILON)
    return (values * inverse, inverse)


def project(gradient, direction, inverse):
    return (gradient - direction * jnp.sum(gradient * direction, axis=1, keepdims=True)) * inverse


class Group:
    def __init__(self, me, size, device_of, order, sems):
        self.me, self.size, self.device_of, self.sems = me, size, device_of, sems
        self.order = order

    def others(self, order=None):
        order = order or self.order
        return [order(self.me, self.size, k) for k in range(1, self.size)]

    def copy(self, src, dst, stage, to, later=None):
        send_sems, recv_sems = self.sems
        return pltpu.make_async_remote_copy(
            src_ref=src,
            dst_ref=dst,
            send_sem=send_sems.at[stage if later is None else later],
            recv_sem=recv_sems.at[stage],
            device_id=self.device_of(to),
            device_id_type=MESH,
        )

    def whole(self, buf, stage):
        part = buf.at[pl.ds(0, self.size - 1)]
        return self.copy(part, part, stage, self.order(self.me, self.size, 1))

    def start_gather(self, buf, stage, order=None):
        mine = buf.at[self.me]
        for to in self.others(order):
            self.copy(mine, mine, stage, to).start()

    def wait_recv(self, buf, stage):
        self.whole(buf, stage).wait_recv()

    def wait_send(self, buf, stage):
        self.whole(buf, stage).wait_send()

    def wait_some(self, buf, stage, count):
        part = buf.at[pl.ds(0, count)]
        self.copy(part, part, stage, self.order(self.me, self.size, 1)).wait_send()

    def start_scatter(self, parts, slots, stage, order=None, part=slice(None), later=None):
        for to in self.others(order)[part]:
            self.copy(parts.at[to], slots.at[self.me], stage, to, later).start()


def ascending(me, size, k):
    return k - 1 + (k - 1 >= me).astype(jnp.int32)


def far_first(me, size, k):
    low = size - k - (size - k <= me).astype(jnp.int32)
    return jnp.where(2 * me < size, low, ascending(me, size, k))


def turned(me, size, k):
    if size & (size - 1):
        return lax.rem(me + k, size)
    out, bit = me, 1
    while bit <= k:
        if k & bit:
            out = out + bit * (1 - 2 * lax.rem(me // bit, 2))
        bit *= 2
    return out


def flipped(me, size, k):
    return turned(me, size, size - k)


def as_column(row):
    size = row.shape[1]
    shape = (size, size)
    same = lax.broadcasted_iota(jnp.int32, shape, 0) == lax.broadcasted_iota(jnp.int32, shape, 1)
    return jnp.sum(jnp.where(same, row, 0.0), axis=1, keepdims=True)


def as_row(column):
    size = column.shape[0]
    shape = (size, size)
    same = lax.broadcasted_iota(jnp.int32, shape, 0) == lax.broadcasted_iota(jnp.int32, shape, 1)
    return jnp.sum(jnp.where(same, column, 0.0), axis=0, keepdims=True)


def merge(stats):
    highest = jnp.max(stats[:, 0:1, :], axis=0)
    total = jnp.sum(stats[:, 1:2, :] * jnp.exp(stats[:, 0:1, :] - highest[None]), axis=0)
    return highest + jnp.log(total)


def flat_half(blocks):
    count, rows, width = blocks.shape
    return blocks.astype(jnp.float32).reshape(count * rows, width).astype(jnp.bfloat16)


def kernel(
    inner_count,
    line_count,
    pair_count,
    scale_ref,
    image_hbm,
    text_hbm,
    loss_ref,
    image_grad_ref,
    text_grad_ref,
    images,
    texts,
    row_stats,
    col_stats,
    row_sums,
    col_sums,
    image_parts,
    text_parts,
    image_slots,
    text_slots,
    image_ref,
    text_ref,
    input_sems,
    line_send,
    line_recv,
    plane_send,
    plane_recv,
):
    text_in = pltpu.make_async_copy(text_hbm, text_ref, input_sems.at[0])
    image_in = pltpu.make_async_copy(image_hbm, image_ref, input_sems.at[1])
    text_in.start()
    image_in.start()
    inner, blk = lax.axis_index("inner"), lax.axis_index("blk")
    place, side = blk // pair_count, lax.rem(blk, pair_count)
    line = Group(
        place,
        line_count,
        lambda z: (inner, z * pair_count + side),
        ascending,
        (line_send, line_recv),
    )
    plane = Group(
        inner * pair_count + side,
        inner_count * pair_count,
        lambda g: (g // pair_count, place * pair_count + lax.rem(g, pair_count)),
        flipped,
        (plane_send, plane_recv),
    )
    barrier = pltpu.get_barrier_semaphore()
    meets = [group.device_of(to) for group in (plane, line) for to in group.others()]
    for to in meets:
        pl.semaphore_signal(barrier, inc=1, device_id=to, device_id_type=MESH)

    factor = scale_ref[0]
    text_in.wait()
    text_unit, text_inverse = unit_rows(text_ref[...])
    text_half = text_unit.astype(jnp.bfloat16)
    texts[plane.me] = text_half
    image_in.wait()
    image_unit, image_inverse = unit_rows(image_ref[...])
    image_half = image_unit.astype(jnp.bfloat16)
    images[line.me] = image_half
    chips = range(1, inner_count)
    near = [k for k in chips if k & (k - 1) == 0] if pair_count == 2 else list(chips)
    far = [k for k in chips if k not in near]
    chip_at = lambda k: turned(inner, inner_count, k)
    slot = lambda g, c: texts.at[g * pair_count + c]

    def text_copy(block, g, c, stage):
        return plane.copy(block, block, stage, g * pair_count + c, 0)

    def start_texts():
        mine = slot(inner, side)
        for k in reversed(far):
            text_copy(mine, chip_at(k), side, 4).start()
        for k in near:
            for c in range(pair_count):
                text_copy(mine, chip_at(k), c, 0).start()
        if pair_count == 2:
            text_copy(mine, inner, 1 - side, 0).start()

    def some(count, stage):
        blocks = texts.at[pl.ds(0, count)]
        return plane.copy(blocks, blocks, stage, inner * pair_count + 1 - side)

    near_blocks = pair_count * len(near) + pair_count - 1

    pl.semaphore_wait(barrier, plane.size + line.size - 2)
    line.start_gather(images, 0, far_first)
    start_texts()
    image_back = image_half.astype(jnp.float32)
    text_back = text_half.astype(jnp.float32)
    diagonal = factor * jnp.sum(image_back * text_back)
    if far:
        some(len(far), 4).wait_recv()
        for k in far:
            text_copy(slot(chip_at(k), side), inner, 1 - side, 5).start()
    some(near_blocks, 0).wait_recv()
    if far:
        some(len(far), 5).wait_recv()
    text_group = flat_half(texts[...])
    line.wait_recv(images, 0)

    image_group = flat_half(images[...])
    image_count, text_count = image_group.shape[0], text_group.shape[0]
    turned_logits = factor * lax.dot_general(
        text_group, image_group, (((1,), (1,)), ((), ())), preferred_element_type=jnp.float32
    )
    row_peak = jnp.max(turned_logits, axis=0, keepdims=True)
    row_total = jnp.sum(jnp.exp(turned_logits - row_peak), axis=0, keepdims=True)
    row_stats[line.me, 0:1, :] = row_peak
    row_stats[line.me, 1:2, :] = row_total
    line.start_gather(row_stats, 1, far_first)
    logits = factor * lax.dot_general(
        image_group, text_group, (((1,), (1,)), ((), ())), preferred_element_type=jnp.float32
    )
    col_peak = jnp.max(logits, axis=0, keepdims=True)
    col_total = jnp.sum(jnp.exp(logits - col_peak), axis=0, keepdims=True)
    col_stats[plane.me, 0:1, :] = col_peak
    col_stats[plane.me, 1:2, :] = col_total
    col_stats[plane.me, 2:3, :] = jnp.full((1, text_count), diagonal, jnp.float32)
    plane.start_gather(col_stats, 1)
    plane.wait_recv(col_stats, 1)
    col_lse = merge(col_stats[...])
    col_weights = jnp.exp(logits - col_lse)
    turned_weights = jnp.exp(turned_logits - as_column(col_lse))
    line.wait_recv(row_stats, 1)
    row_lse = merge(row_stats[...])

    weights = (
        0.5 * factor * (jnp.exp(logits - as_column(row_lse)) + col_weights)
    ).astype(jnp.bfloat16)
    image_parts[...] = (
        jnp.dot(weights, text_group, preferred_element_type=jnp.float32)
        .reshape(image_parts.shape)
        .astype(jnp.bfloat16)
    )
    line.start_scatter(image_parts, image_slots, 2, part=slice(0, 1))
    turned_weights = (
        0.5 * factor * (jnp.exp(turned_logits - row_lse) + turned_weights)
    ).astype(jnp.bfloat16)
    text_parts[...] = (
        jnp.dot(turned_weights, image_group, preferred_element_type=jnp.float32)
        .reshape(text_parts.shape)
        .astype(jnp.bfloat16)
    )
    plane.start_scatter(text_parts, text_slots, 2, ascending, slice(0, pair_count))
    tile = row_sums.shape[1:]
    plane_diagonal = jnp.sum(col_stats[:, 2, 0:1])
    row_sums[plane.me] = jnp.full(tile, jnp.sum(row_lse), jnp.float32)
    col_sums[line.me] = jnp.full(tile, jnp.sum(col_lse) - 2.0 * plane_diagonal, jnp.float32)
    plane.start_gather(row_sums, 3)
    line.start_gather(col_sums, 3)

    held = place == line_count - 1

    @pl.when(held)
    def _():
        line.wait_some(image_parts, 2, 1)

    line.start_scatter(image_parts, image_slots, 2, part=slice(1, None), later=4)
    plane.start_scatter(text_parts, text_slots, 2, ascending, slice(pair_count, None), 4)

    rows = image_ref.shape[0]
    line.wait_recv(image_slots, 2)
    image_sum = image_parts[line.me].astype(jnp.float32)
    for other in line.others():
        image_sum = image_sum + image_slots[other].astype(jnp.float32)
    image_grad_ref[...] = project(image_sum - factor * text_back, image_unit, image_inverse)
    plane.wait_recv(text_slots, 2)
    text_sum = text_parts[plane.me].astype(jnp.float32)
    for other in plane.others():
        text_sum = text_sum + text_slots[other].astype(jnp.float32)
    text_grad_ref[...] = project(text_sum - factor * image_back, text_unit, text_inverse)

    plane.wait_recv(row_sums, 3)
    line.wait_recv(col_sums, 3)
    examples = 2.0 * line.size * plane.size * rows
    whole = jnp.sum(row_sums[...], axis=0)[0:1, 0:1] + jnp.sum(col_sums[...], axis=0)[0:1, 0:1]
    loss_ref[...] = jnp.broadcast_to(whole / examples, loss_ref.shape)
    plane.wait_some(text_parts, 2, pair_count)

    @pl.when(jnp.logical_not(held))
    def _():
        line.wait_some(image_parts, 2, 1)

    line.wait_some(image_parts, 4, line_count - 2)
    plane.wait_some(text_parts, 4, plane.size - 1 - pair_count)
    line.wait_send(images, 0)
    some(near_blocks + 2 * len(far), 0).wait_send()
    for buf_line, buf_plane, stage in (
        (row_stats, col_stats, 1),
        (col_sums, row_sums, 3),
    ):
        line.wait_send(buf_line, stage)
        plane.wait_send(buf_plane, stage)


def store(loss, image_grad, text_grad, loss_hbm, image_hbm, text_hbm, sems):
    pairs = ((image_grad, image_hbm), (text_grad, text_hbm), (loss, loss_hbm))
    copies = [pltpu.make_async_copy(*pair, sems.at[k]) for k, pair in enumerate(pairs)]
    for copy in copies:
        copy.start()
    for copy in copies:
        copy.wait()


def solution(mesh):
    inner_count, blk_count = mesh.shape["inner"], mesh.shape["blk"]
    pair_count = 2 if blk_count % 2 == 0 else 1
    line_count = blk_count // pair_count
    plane_count = inner_count * pair_count

    def on_device(image_emb, text_emb, logit_scale):
        rows, width = image_emb.shape
        vmem = pl.BlockSpec(memory_space=pltpu.VMEM)
        hbm = pl.BlockSpec(memory_space=pl.ANY)
        smem = pl.BlockSpec(memory_space=pltpu.SMEM)
        near = pltpu.VMEM((rows, width), jnp.float32)
        results = pl.pallas_call(
            functools.partial(kernel, inner_count, line_count, pair_count),
            out_shape=(pltpu.VMEM((1, 128), jnp.float32), near, near),
            in_specs=[smem, hbm, hbm],
            out_specs=(vmem, vmem, vmem),
            scratch_shapes=[
                pltpu.VMEM((line_count, rows, width), jnp.bfloat16),
                pltpu.VMEM((plane_count, rows, width), jnp.bfloat16),
                pltpu.VMEM((line_count, 2, line_count * rows), jnp.float32),
                pltpu.VMEM((plane_count, 4, plane_count * rows), jnp.float32),
                pltpu.VMEM((plane_count, 1, 128), jnp.float32),
                pltpu.VMEM((line_count, 1, 128), jnp.float32),
                pltpu.VMEM((line_count, rows, width), jnp.bfloat16),
                pltpu.VMEM((plane_count, rows, width), jnp.bfloat16),
                pltpu.VMEM((line_count, rows, width), jnp.bfloat16),
                pltpu.VMEM((plane_count, rows, width), jnp.bfloat16),
                pltpu.VMEM((rows, width), jnp.float32),
                pltpu.VMEM((rows, width), jnp.float32),
                pltpu.SemaphoreType.DMA((2,)),
                pltpu.SemaphoreType.DMA((5,)),
                pltpu.SemaphoreType.DMA((4,)),
                pltpu.SemaphoreType.DMA((5,)),
                pltpu.SemaphoreType.DMA((6,)),
            ],
            compiler_params=pltpu.CompilerParams(
                collective_id=0, has_side_effects=True, vmem_limit_bytes=56 * 1024 * 1024
            ),
            name="contrastive",
        )(logit_scale, image_emb, text_emb)
        far = jax.ShapeDtypeStruct((rows, width), jnp.float32)
        loss, image_grad, text_grad = pl.pallas_call(
            store,
            out_shape=(jax.ShapeDtypeStruct((1, 128), jnp.float32), far, far),
            in_specs=[vmem, vmem, vmem],
            out_specs=(hbm, hbm, hbm),
            scratch_shapes=[pltpu.SemaphoreType.DMA((3,))],
            compiler_params=pltpu.CompilerParams(vmem_limit_bytes=16 * 1024 * 1024),
            name="store",
        )(*results)
        return loss.reshape(128)[0:1], image_grad, text_grad

    in_specs = (P(("inner", "blk"), None), P(("inner", "blk"), None), P())
    out_specs = (P(), P(("inner", "blk"), None), P(("inner", "blk"), None))
    return jax.shard_map(
        on_device, mesh=mesh, in_specs=in_specs, out_specs=out_specs, check_vma=False
    )
```

```python
import functools

import jax
import jax.numpy as jnp
from jax import lax
from jax.experimental import pallas as pl
from jax.experimental.pallas import tpu as pltpu
from jax.sharding import PartitionSpec as P

EPSILON = 1e-06
MESH = pl.DeviceIdType.MESH


def unit_rows(values):
    inverse = lax.rsqrt(jnp.sum(values * values, axis=1, keepdims=True) + EPSILON)
    return (values * inverse, inverse)


def project(gradient, direction, inverse):
    return (gradient - direction * jnp.sum(gradient * direction, axis=1, keepdims=True)) * inverse


class Group:
    def __init__(self, me, size, device_of, order, sems):
        self.me, self.size, self.device_of, self.sems = me, size, device_of, sems
        self.order = order

    def others(self, order=None):
        order = order or self.order
        return [order(self.me, self.size, k) for k in range(1, self.size)]

    def copy(self, src, dst, stage, to, later=None):
        send_sems, recv_sems = self.sems
        return pltpu.make_async_remote_copy(
            src_ref=src,
            dst_ref=dst,
            send_sem=send_sems.at[stage if later is None else later],
            recv_sem=recv_sems.at[stage],
            device_id=self.device_of(to),
            device_id_type=MESH,
        )

    def whole(self, buf, stage):
        part = buf.at[pl.ds(0, self.size - 1)]
        return self.copy(part, part, stage, self.order(self.me, self.size, 1))

    def start_gather(self, buf, stage, order=None):
        mine = buf.at[self.me]
        for to in self.others(order):
            self.copy(mine, mine, stage, to).start()

    def wait_recv(self, buf, stage):
        self.whole(buf, stage).wait_recv()

    def wait_send(self, buf, stage):
        self.whole(buf, stage).wait_send()

    def wait_some(self, buf, stage, count):
        part = buf.at[pl.ds(0, count)]
        self.copy(part, part, stage, self.order(self.me, self.size, 1)).wait_send()

    def start_scatter(self, parts, slots, stage, order=None, part=slice(None), later=None):
        for to in self.others(order)[part]:
            self.copy(parts.at[to], slots.at[self.me], stage, to, later).start()


def ascending(me, size, k):
    return k - 1 + (k - 1 >= me).astype(jnp.int32)


def far_first(me, size, k):
    low = size - k - (size - k <= me).astype(jnp.int32)
    return jnp.where(2 * me < size, low, ascending(me, size, k))


def turned(me, size, k):
    if size & (size - 1):
        return lax.rem(me + k, size)
    out, bit = me, 1
    while bit <= k:
        if k & bit:
            out = out + bit * (1 - 2 * lax.rem(me // bit, 2))
        bit *= 2
    return out


def flipped(me, size, k):
    return turned(me, size, size - k)


def as_column(row):
    size = row.shape[1]
    shape = (size, size)
    same = lax.broadcasted_iota(jnp.int32, shape, 0) == lax.broadcasted_iota(jnp.int32, shape, 1)
    return jnp.sum(jnp.where(same, row, 0.0), axis=1, keepdims=True)


def as_row(column):
    size = column.shape[0]
    shape = (size, size)
    same = lax.broadcasted_iota(jnp.int32, shape, 0) == lax.broadcasted_iota(jnp.int32, shape, 1)
    return jnp.sum(jnp.where(same, column, 0.0), axis=0, keepdims=True)


def merge(stats):
    highest = jnp.max(stats[:, 0:1, :], axis=0)
    total = jnp.sum(stats[:, 1:2, :] * jnp.exp(stats[:, 0:1, :] - highest[None]), axis=0)
    return highest + jnp.log(total)


def flat_half(blocks):
    count, rows, width = blocks.shape
    return blocks.astype(jnp.float32).reshape(count * rows, width).astype(jnp.bfloat16)


def kernel(
    inner_count,
    line_count,
    pair_count,
    scale_ref,
    image_hbm,
    text_hbm,
    loss_ref,
    image_grad_ref,
    text_grad_ref,
    images,
    texts,
    row_stats,
    col_stats,
    row_sums,
    col_sums,
    image_parts,
    text_parts,
    image_slots,
    text_slots,
    image_ref,
    text_ref,
    input_sems,
    line_send,
    line_recv,
    plane_send,
    plane_recv,
):
    text_in = pltpu.make_async_copy(text_hbm, text_ref, input_sems.at[0])
    image_in = pltpu.make_async_copy(image_hbm, image_ref, input_sems.at[1])
    text_in.start()
    image_in.start()
    inner, blk = lax.axis_index("inner"), lax.axis_index("blk")
    place, side = blk // pair_count, lax.rem(blk, pair_count)
    line = Group(
        place,
        line_count,
        lambda z: (inner, z * pair_count + side),
        ascending,
        (line_send, line_recv),
    )
    plane = Group(
        inner * pair_count + side,
        inner_count * pair_count,
        lambda g: (g // pair_count, place * pair_count + lax.rem(g, pair_count)),
        flipped,
        (plane_send, plane_recv),
    )
    barrier = pltpu.get_barrier_semaphore()
    meets = [group.device_of(to) for group in (plane, line) for to in group.others()]
    for to in meets:
        pl.semaphore_signal(barrier, inc=1, device_id=to, device_id_type=MESH)

    factor = scale_ref[0]
    text_in.wait()
    text_unit, text_inverse = unit_rows(text_ref[...])
    text_half = text_unit.astype(jnp.bfloat16)
    texts[plane.me] = text_half
    image_in.wait()
    image_unit, image_inverse = unit_rows(image_ref[...])
    image_half = image_unit.astype(jnp.bfloat16)
    images[line.me] = image_half
    chips = range(1, inner_count)
    near = [k for k in chips if k & (k - 1) == 0] if pair_count == 2 else list(chips)
    far = [k for k in chips if k not in near]
    chip_at = lambda k: turned(inner, inner_count, k)
    slot = lambda g, c: texts.at[g * pair_count + c]

    def text_copy(block, g, c, stage):
        return plane.copy(block, block, stage, g * pair_count + c, 0)

    def start_texts():
        mine = slot(inner, side)
        for k in reversed(far):
            text_copy(mine, chip_at(k), side, 4).start()
        for k in near:
            for c in range(pair_count):
                text_copy(mine, chip_at(k), c, 0).start()
        if pair_count == 2:
            text_copy(mine, inner, 1 - side, 0).start()

    def some(count, stage):
        blocks = texts.at[pl.ds(0, count)]
        return plane.copy(blocks, blocks, stage, inner * pair_count + 1 - side)

    near_blocks = pair_count * len(near) + pair_count - 1

    pl.semaphore_wait(barrier, plane.size + line.size - 2)
    line.start_gather(images, 0, far_first)
    start_texts()
    image_back = image_half.astype(jnp.float32)
    text_back = text_half.astype(jnp.float32)
    diagonal = factor * jnp.sum(image_back * text_back)
    if far:
        some(len(far), 4).wait_recv()
        for k in far:
            text_copy(slot(chip_at(k), side), inner, 1 - side, 5).start()
    some(near_blocks, 0).wait_recv()
    if far:
        some(len(far), 5).wait_recv()
    text_group = flat_half(texts[...])
    line.wait_recv(images, 0)

    image_group = flat_half(images[...])
    image_count, text_count = image_group.shape[0], text_group.shape[0]
    turned_logits = factor * lax.dot_general(
        text_group, image_group, (((1,), (1,)), ((), ())), preferred_element_type=jnp.float32
    )
    row_peak = jnp.max(turned_logits, axis=0, keepdims=True)
    row_total = jnp.sum(jnp.exp(turned_logits - row_peak), axis=0, keepdims=True)
    row_stats[line.me, 0:1, :] = row_peak
    row_stats[line.me, 1:2, :] = row_total
    line.start_gather(row_stats, 1, far_first)
    logits = factor * lax.dot_general(
        image_group, text_group, (((1,), (1,)), ((), ())), preferred_element_type=jnp.float32
    )
    col_peak = jnp.max(logits, axis=0, keepdims=True)
    col_total = jnp.sum(jnp.exp(logits - col_peak), axis=0, keepdims=True)
    col_stats[plane.me, 0:1, :] = col_peak
    col_stats[plane.me, 1:2, :] = col_total
    col_stats[plane.me, 2:3, :] = jnp.full((1, text_count), diagonal, jnp.float32)
    plane.start_gather(col_stats, 1)
    plane.wait_recv(col_stats, 1)
    col_lse = merge(col_stats[...])
    col_weights = jnp.exp(logits - col_lse)
    turned_weights = jnp.exp(turned_logits - as_column(col_lse))
    line.wait_recv(row_stats, 1)
    row_lse = merge(row_stats[...])

    tile = row_sums.shape[1:]
    plane_diagonal = jnp.sum(col_stats[:, 2, 0:1])
    row_sums[plane.me] = jnp.full(tile, jnp.sum(row_lse), jnp.float32)
    col_sums[line.me] = jnp.full(tile, jnp.sum(col_lse) - 2.0 * plane_diagonal, jnp.float32)
    plane.start_gather(row_sums, 3)
    line.start_gather(col_sums, 3)

    weights = (
        0.5 * factor * (jnp.exp(logits - as_column(row_lse)) + col_weights)
    ).astype(jnp.bfloat16)
    image_parts[...] = (
        jnp.dot(weights, text_group, preferred_element_type=jnp.float32)
        .reshape(image_parts.shape)
        .astype(jnp.bfloat16)
    )
    line.start_scatter(image_parts, image_slots, 2, part=slice(0, 1))
    turned_weights = (
        0.5 * factor * (jnp.exp(turned_logits - row_lse) + turned_weights)
    ).astype(jnp.bfloat16)
    text_parts[...] = (
        jnp.dot(turned_weights, image_group, preferred_element_type=jnp.float32)
        .reshape(text_parts.shape)
        .astype(jnp.bfloat16)
    )
    plane.start_scatter(text_parts, text_slots, 2, ascending, slice(0, pair_count))
    held = place == line_count - 1

    @pl.when(held)
    def _():
        line.wait_some(image_parts, 2, 1)

    line.start_scatter(image_parts, image_slots, 2, part=slice(1, None), later=4)
    plane.start_scatter(text_parts, text_slots, 2, ascending, slice(pair_count, None), 4)

    rows = image_ref.shape[0]
    plane.wait_recv(text_slots, 2)
    text_sum = text_parts[plane.me].astype(jnp.float32)
    for other in plane.others():
        text_sum = text_sum + text_slots[other].astype(jnp.float32)
    text_grad_ref[...] = project(text_sum - factor * image_back, text_unit, text_inverse)
    line.wait_recv(image_slots, 2)
    image_sum = image_parts[line.me].astype(jnp.float32)
    for other in line.others():
        image_sum = image_sum + image_slots[other].astype(jnp.float32)
    image_grad_ref[...] = project(image_sum - factor * text_back, image_unit, image_inverse)

    plane.wait_recv(row_sums, 3)
    line.wait_recv(col_sums, 3)
    examples = 2.0 * line.size * plane.size * rows
    whole = jnp.sum(row_sums[...], axis=0)[0:1, 0:1] + jnp.sum(col_sums[...], axis=0)[0:1, 0:1]
    loss_ref[...] = jnp.broadcast_to(whole / examples, loss_ref.shape)
    plane.wait_some(text_parts, 2, pair_count)

    @pl.when(jnp.logical_not(held))
    def _():
        line.wait_some(image_parts, 2, 1)

    line.wait_some(image_parts, 4, line_count - 2)
    plane.wait_some(text_parts, 4, plane.size - 1 - pair_count)
    line.wait_send(images, 0)
    some(near_blocks + 2 * len(far), 0).wait_send()
    for buf_line, buf_plane, stage in (
        (row_stats, col_stats, 1),
        (col_sums, row_sums, 3),
    ):
        line.wait_send(buf_line, stage)
        plane.wait_send(buf_plane, stage)


def store(loss, image_grad, text_grad, loss_hbm, image_hbm, text_hbm, sems):
    pairs = ((image_grad, image_hbm), (text_grad, text_hbm), (loss, loss_hbm))
    copies = [pltpu.make_async_copy(*pair, sems.at[k]) for k, pair in enumerate(pairs)]
    for copy in copies:
        copy.start()
    for copy in copies:
        copy.wait()


def solution(mesh):
    inner_count, blk_count = mesh.shape["inner"], mesh.shape["blk"]
    pair_count = 2 if blk_count % 2 == 0 else 1
    line_count = blk_count // pair_count
    plane_count = inner_count * pair_count

    def on_device(image_emb, text_emb, logit_scale):
        rows, width = image_emb.shape
        vmem = pl.BlockSpec(memory_space=pltpu.VMEM)
        hbm = pl.BlockSpec(memory_space=pl.ANY)
        smem = pl.BlockSpec(memory_space=pltpu.SMEM)
        near = pltpu.VMEM((rows, width), jnp.float32)
        results = pl.pallas_call(
            functools.partial(kernel, inner_count, line_count, pair_count),
            out_shape=(pltpu.VMEM((1, 128), jnp.float32), near, near),
            in_specs=[smem, hbm, hbm],
            out_specs=(vmem, vmem, vmem),
            scratch_shapes=[
                pltpu.VMEM((line_count, rows, width), jnp.bfloat16),
                pltpu.VMEM((plane_count, rows, width), jnp.bfloat16),
                pltpu.VMEM((line_count, 2, line_count * rows), jnp.float32),
                pltpu.VMEM((plane_count, 4, plane_count * rows), jnp.float32),
                pltpu.VMEM((plane_count, 1, 128), jnp.float32),
                pltpu.VMEM((line_count, 1, 128), jnp.float32),
                pltpu.VMEM((line_count, rows, width), jnp.bfloat16),
                pltpu.VMEM((plane_count, rows, width), jnp.bfloat16),
                pltpu.VMEM((line_count, rows, width), jnp.bfloat16),
                pltpu.VMEM((plane_count, rows, width), jnp.bfloat16),
                pltpu.VMEM((rows, width), jnp.float32),
                pltpu.VMEM((rows, width), jnp.float32),
                pltpu.SemaphoreType.DMA((2,)),
                pltpu.SemaphoreType.DMA((5,)),
                pltpu.SemaphoreType.DMA((4,)),
                pltpu.SemaphoreType.DMA((5,)),
                pltpu.SemaphoreType.DMA((6,)),
            ],
            compiler_params=pltpu.CompilerParams(
                collective_id=0, has_side_effects=True, vmem_limit_bytes=56 * 1024 * 1024
            ),
            name="contrastive",
        )(logit_scale, image_emb, text_emb)
        far = jax.ShapeDtypeStruct((rows, width), jnp.float32)
        loss, image_grad, text_grad = pl.pallas_call(
            store,
            out_shape=(jax.ShapeDtypeStruct((1, 128), jnp.float32), far, far),
            in_specs=[vmem, vmem, vmem],
            out_specs=(hbm, hbm, hbm),
            scratch_shapes=[pltpu.SemaphoreType.DMA((3,))],
            compiler_params=pltpu.CompilerParams(vmem_limit_bytes=16 * 1024 * 1024),
            name="store",
        )(*results)
        return loss.reshape(128)[0:1], image_grad, text_grad

    in_specs = (P(("inner", "blk"), None), P(("inner", "blk"), None), P())
    out_specs = (P(), P(("inner", "blk"), None), P(("inner", "blk"), None))
    return jax.shard_map(
        on_device, mesh=mesh, in_specs=in_specs, out_specs=out_specs, check_vma=False
    )
```
